32 devices in a mesh: space: 16 (over z, x, core), port: 2 (over y).
Axes of the slice: x: 2, y: 2, z: 4, core: 2. Of those that a mesh axis runs over, the one named last changes fastest.
Arguments:
- fields: float32 [2, 2, 6, 64, 64, 128], P(None, 'port', None, 'space'), may hold values from -6 to 6
- inv_eps: float32 [3, 64, 64, 128], P(None, 'space'), may hold values from 0.04 to 0.48
- tensor_tiles: float32 [16, 16, 24, 128], P('space'), may hold values from -0.08 to 0.32
- tile_index: int32 [16, 16, 4], P('space'), may hold values from -1 to 255, as said below
- ports: int32 [2, 2], replicated, may hold values from 0 to 524287
- waves: float32 [2, 2, 8], P(None, 'port'), may hold values from -8 to 8
Outputs:
- fields_out: float32 [2, 2, 6, 64, 64, 128], P(None, 'port', None, 'space')
- sensitivity: float32 [64, 64, 128], P('space', 'port')
The draws below stay inside these ranges and needn't reach their ends.
Inputs may be any that keep to these rules, and one draw needn't show every extreme that they name: tile_index[d, s, k] is -1 for an empty slot or a column number j of slab d (x-major); no number repeats within one slab's lists; the live slots of one owner come first; every owner has one or more live slots for every slab; slot 0 from owner 0 of every slab holds the column 255; some slab gets all 4 slots live from every owner.
All inputs are finite; a program needn't handle non-finite values.
Results may differ from the reference program's by a relative error of at most 0.0003.
Values sent between devices are 32-bit elements; how exact they have to be, the bound alone decides.
A program may use at most 64 MiB of HBM per device.

```python
import math
import jax
import jax.numpy as jnp
from jax import lax

CX = 4
NY = 64
NZ = 128
STEPS = 8
CAP = 4
SLABS = 16
NX = 64
PORTS = 2


def draw_tensor_tiles(key, part):
    first, second, third = jax.random.split(key, 3)
    shape = (SLABS, SLABS, CAP, 6, NZ)
    entry = jnp.arange(6).reshape(1, 1, 1, 6, 1)
    diagonal = jax.random.uniform(first, shape, jnp.float32, 0.2, 0.3)
    magnitude = jax.random.uniform(second, shape, jnp.float32, 0.02, 0.08)
    signs = jnp.where(jax.random.bernoulli(third, 0.5, shape), 1.0, -1.0)
    values = jnp.where(entry < 3, diagonal, signs * magnitude)
    return values.reshape(SLABS, SLABS, CAP * 6, NZ).astype(jnp.float32)


def draw_tile_index(key, part):
    keys = jax.random.split(key, 5)
    heavy = jax.random.randint(keys[0], (SLABS,), 0, 2)
    light_count = jax.random.randint(keys[1], (SLABS, SLABS), 1, 3)
    heavy_count = jax.random.randint(keys[2], (SLABS, SLABS), 1, CAP + 1)
    counts = jnp.where(heavy[None, :] == 1, heavy_count, light_count)
    full_slab = jax.random.randint(keys[3], (), 0, SLABS)
    counts = jnp.where(jnp.arange(SLABS)[None, :] == full_slab, CAP, counts)
    counts = jnp.minimum(counts, CAP)
    offsets = jnp.cumsum(counts, axis=0) - counts
    column_total = CX * NY
    raw_orders = jax.vmap(lambda sub_key: jax.random.permutation(sub_key, column_total))(jax.random.split(keys[4], SLABS))
    orders = (raw_orders - raw_orders[:, :1] - 1) % column_total
    slot_ids = jnp.arange(CAP)[None, None, :]
    ranks = jnp.minimum(offsets[:, :, None] + slot_ids, column_total - 1)
    chosen = orders[jnp.arange(SLABS)[None, :, None], ranks]
    live = slot_ids < counts[:, :, None]
    result = jnp.where(live, chosen, -1)
    return result.transpose(1, 0, 2).astype(jnp.int32)


def plant(entries, key, low, high):
    longest = entries.shape.index(max(entries.shape))
    spots = []
    for shift in (0, 1):
        where = [jax.random.randint(jax.random.fold_in(key, axis), (), 0, length) for axis, length in enumerate(entries.shape)]
        where[longest] = (where[longest] + shift) % entries.shape[longest]
        spots.append(tuple(where))
    return entries.at[spots[0]].set(low).at[spots[1]].set(high)


def levels(rng, extent, cuts, low, high):
    gain, own = 1.0, jax.random.fold_in(rng, 6)
    for position, parts in cuts:
        steps = jnp.exp(jax.random.uniform(jax.random.fold_in(own, position), (parts,), jnp.float32, low / len(cuts), high / len(cuts)))
        gain = gain * jnp.repeat(steps, extent[position] // parts).reshape([-1 if axis == position else 1 for axis in range(len(extent))])
    return gain


def scatter_about(rng, shape, width, most, cuts=(), held_as=jnp.bfloat16):
    entries = jax.random.normal(rng, shape, jnp.float32) * width
    if len(cuts) > 0:
        entries = levels(rng, shape, cuts, -0.22, 0.18) * entries
    return jnp.clip(entries, min=-most, max=most).astype(held_as)


def setup_inputs(seed: int = 0) -> dict:
    seeds = jax.random.split(jax.random.key(seed), 7)
    fields = scatter_about(seeds[0], (2, PORTS, 6, NX, NY, NZ), 1.0, 6.0, ((1, 2), (3, 16)), jnp.float32)
    inv_eps = jnp.clip(jnp.exp(math.log(0.48) - 2.4849066 * jax.random.uniform(seeds[1], (3, NX, NY, NZ), jnp.float32) ** levels(seeds[1], (3, NX, NY, NZ), ((1, 16),), -0.2, 0.2)), 0.04, 0.48)
    tensor_tiles = draw_tensor_tiles(jax.random.fold_in(seeds[6], 71), 0)
    tile_index = draw_tile_index(jax.random.fold_in(seeds[6], 71), 0)
    ports = plant(jax.random.randint(seeds[4], (2, PORTS), 0, NX * NY * NZ), jax.random.fold_in(seeds[4], 1), 0, (NX * NY * NZ) - 1).astype(jnp.int32)
    waves = scatter_about(seeds[5], (2, PORTS, STEPS), 2.0, 8.0, ((1, 2),), jnp.float32)
    return {"fields": fields, "inv_eps": inv_eps, "tensor_tiles": tensor_tiles, "tile_index": tile_index, "ports": ports, "waves": waves}


magnetic_coef = 0.5

def forward_cell(values, along):
    widths = [(0, 0)] * values.ndim
    widths[along] = (0, 1)
    return lax.slice_in_dim(jnp.pad(values, widths), 1, values.shape[along] + 1, axis=along)

def backward_cell(values, along):
    widths = [(0, 0)] * values.ndim
    widths[along] = (1, 0)
    return lax.slice_in_dim(jnp.pad(values, widths), 0, values.shape[along], axis=along)

def magnetic_update(magnetic, electric, elec_y_up, elec_z_up):
    elec_x, elec_y, elec_z = (electric[:, 0], electric[:, 1], electric[:, 2])
    magn_x = magnetic[:, 0] - magnetic_coef * (forward_cell(elec_z, 2) - elec_z - (forward_cell(elec_y, 3) - elec_y))
    magn_y = magnetic[:, 1] - magnetic_coef * (forward_cell(elec_x, 3) - elec_x - (elec_z_up - elec_z))
    magn_z = magnetic[:, 2] - magnetic_coef * (elec_y_up - elec_y - (forward_cell(elec_x, 2) - elec_x))
    return jnp.stack([magn_x, magn_y, magn_z], 1)

def electric_update(electric, magnetic, magn_y_down, magn_z_down, tensor):
    magn_x, magn_y, magn_z = (magnetic[:, 0], magnetic[:, 1], magnetic[:, 2])
    curl_x = magn_z - backward_cell(magn_z, 2) - (magn_y - backward_cell(magn_y, 3))
    curl_y = magn_x - backward_cell(magn_x, 3) - (magn_z - magn_z_down)
    curl_z = magn_y - magn_y_down - (magn_x - backward_cell(magn_x, 2))
    elec_x = electric[:, 0] + (tensor[0] * curl_x + tensor[3] * curl_y + tensor[4] * curl_z)
    elec_y = electric[:, 1] + (tensor[3] * curl_x + tensor[1] * curl_y + tensor[5] * curl_z)
    elec_z = electric[:, 2] + (tensor[4] * curl_x + tensor[5] * curl_y + tensor[2] * curl_z)
    return (elec_x, elec_y, elec_z)

def build_tensor(inv_eps, tensor_tiles, tile_index):
    bulk = jnp.concatenate([inv_eps, jnp.zeros_like(inv_eps)], 0).reshape(6, NX * NY, NZ)
    tiles = tensor_tiles.reshape(SLABS, SLABS, CAP, 6, NZ).transpose(1, 0, 2, 3, 4)
    owner = jnp.arange(SLABS).astype(jnp.int32).reshape(SLABS, 1, 1)
    columns = jnp.where(tile_index >= 0, owner * (CX * NY) + tile_index, NX * NY).astype(jnp.int32)
    rows_in = tiles.reshape(SLABS * SLABS * CAP, 6, NZ).transpose(1, 0, 2)
    bulk = bulk.at[:, columns.reshape(-1)].set(rows_in, mode='drop')
    return bulk.reshape(6, NX, NY, NZ)

def reference(fields, inv_eps, tensor_tiles, tile_index, ports, waves):
    tensor = build_tensor(inv_eps, tensor_tiles, tile_index)
    plane = NY * NZ

    def one_port(inputs):
        start, source_cells, pulses = inputs
        electric = start[:, :3]
        magnetic = start[:, 3:]
        cell_x = (source_cells // plane).astype(jnp.int32)
        cell_y = (source_cells % plane // NZ).astype(jnp.int32)
        cell_z = (source_cells % NZ).astype(jnp.int32)
        sim_ids = jnp.arange(2).astype(jnp.int32)
        summed = jnp.zeros((NX, NY, NZ), jnp.float32)
        for time_step in range(STEPS):
            magnetic = magnetic_update(magnetic, electric, forward_cell(electric[:, 1], 1), forward_cell(electric[:, 2], 1))
            elec_x, elec_y, elec_z = electric_update(electric, magnetic, backward_cell(magnetic[:, 1], 1), backward_cell(magnetic[:, 2], 1), tensor)
            elec_z = elec_z.at[sim_ids, cell_x, cell_y, cell_z].add(pulses[:, time_step])
            summed = summed + (elec_x[0] * elec_x[1] + elec_y[0] * elec_y[1] + elec_z[0] * elec_z[1])
            electric = jnp.stack([elec_x, elec_y, elec_z], 1)
        return (jnp.concatenate([electric, magnetic], 1), summed)
    finals, summed_all = lax.map(one_port, (fields.transpose(1, 0, 2, 3, 4, 5), ports.T, waves.transpose(1, 0, 2)))
    fields_out = finals.transpose(1, 0, 2, 3, 4, 5)
    correlation = lax.optimization_barrier(jnp.sum(summed_all, axis=0))
    sensitivity = correlation * (1.0 / math.sqrt(PORTS * STEPS))
    return (fields_out, sensitivity)
```

```python
import functools
import math

import jax
import jax.numpy as jnp
from jax import lax
from jax.experimental import pallas as pl
from jax.experimental.pallas import tpu as pltpu
from jax.sharding import PartitionSpec as P

MESH = pl.DeviceIdType.MESH
magnetic_coef = 0.5
PAD = 8
ROWS = 16
FAR_ROWS = 16


def kernel(
    slabs, port_devices, ports_in, waves_in, fields, inv_eps, tiles, tile_index,
    elec, magn, result,
    ports_ref, waves_ref, face_up, face_down, partial, tensor, bulk, arrived, index, onehot, live, summed,
    shares, load_sem, tile_send, tile_recv, up_send, up_recv, down_send, down_recv,
    share_send, share_recv,
):
    me = lax.axis_index("space")
    port = lax.axis_index("port")
    width_x, width_y, width_z = inv_eps.shape[1:]
    steps = waves_ref.shape[2]
    last = width_x - 1
    owner_rows = tiles.shape[2]
    slots = owner_rows // 6
    share_rows = width_y // port_devices
    has_below = me > 0
    has_above = me < slabs - 1
    above = jnp.minimum(me + 1, slabs - 1)
    below = jnp.maximum(me - 1, 0)

    def owner_span(owner):
        return pl.ds(pl.multiple_of(owner * owner_rows, 8), owner_rows)

    loads = [
        pltpu.make_async_copy(fields.at[:, 0, pl.ds(0, 3)], elec.at[:, :, :, pl.ds(0, width_y)], load_sem.at[0]),
        pltpu.make_async_copy(fields.at[:, 0, pl.ds(3, 3)], magn.at[:, :, :, pl.ds(PAD, width_y)], load_sem.at[1]),
        pltpu.make_async_copy(inv_eps, bulk, load_sem.at[2]),
        pltpu.make_async_copy(tile_index.at[0], index, load_sem.at[3]),
        pltpu.make_async_copy(tiles.at[0, me], arrived.at[owner_span(me)], load_sem.at[4]),
        pltpu.make_async_copy(ports_in, ports_ref, load_sem.at[5]),
        pltpu.make_async_copy(waves_in, waves_ref, load_sem.at[6]),
    ]
    for load in (loads[3], loads[5], loads[6], loads[0], loads[1], loads[2], loads[4]):
        load.start()

    barrier = pltpu.get_barrier_semaphore()

    def greet(k, carry):
        pl.semaphore_signal(barrier, inc=1, device_id=(lax.rem(me + k, slabs), port), device_id_type=MESH)
        return carry

    def greet_port(k, carry):
        pl.semaphore_signal(barrier, inc=1, device_id=(me, lax.rem(port + k, port_devices)), device_id_type=MESH)
        return carry

    lax.fori_loop(1, slabs, greet, 0)
    lax.fori_loop(1, port_devices, greet_port, 0)

    def up_copy(step, sim, lo, rows):
        span, k = pl.ds(lo, rows), lo // rows
        return pltpu.make_async_remote_copy(
            partial.at[sim, :, span], face_down.at[step, sim, :, span],
            up_send.at[sim, k], up_recv.at[step, sim, k], device_id=(above, port), device_id_type=MESH)

    def down_copy(step, sim, lo, rows, source=None):
        span, k = pl.ds(lo, rows), lo // rows
        if source is None:
            source = elec.at[sim, pl.ds(1, 2), 0, span]
        return pltpu.make_async_remote_copy(
            source, face_up.at[step, sim, :, span],
            down_send.at[sim, k], down_recv.at[step, sim, k], device_id=(below, port), device_id_type=MESH)

    top_is_far = lax.rem(me, 2) == 1

    def by_side(odd, even):
        pl.when(top_is_far)(odd)
        pl.when(jnp.logical_not(top_is_far))(even)

    def pieces(rows):
        return range(0, width_y, rows)

    def tile_copy(k):
        target = lax.rem(me + k, slabs)
        return pltpu.make_async_remote_copy(
            tiles.at[0, target], arrived.at[owner_span(me)],
            tile_send.at[k], tile_recv.at[k], device_id=(target, port), device_id_type=MESH)

    zero_rows = jnp.zeros((PAD, width_z), jnp.float32)
    for sim in range(2):
        for comp in range(3):
            for layer in range(width_x):
                elec[sim, comp, layer, pl.ds(width_y, PAD)] = zero_rows
                magn[sim, comp, layer, pl.ds(0, PAD)] = zero_rows
    zero_plane = jnp.zeros((width_y, width_z), jnp.float32)

    @pl.when(me == 0)
    def _():
        def clear(step, carry):
            for sim in range(2):
                for comp in range(2):
                    face_down[step, sim, comp] = zero_plane
            return carry
        lax.fori_loop(0, steps, clear, 0)

    @pl.when(me == slabs - 1)
    def _():
        def clear(step, carry):
            for sim in range(2):
                for comp in range(2):
                    face_up[step, sim, comp] = zero_plane
            return carry
        lax.fori_loop(0, steps, clear, 0)

    for layer in range(width_x):
        summed[layer] = zero_plane

    columns = width_x * width_y
    loads[3].wait()
    spots_down = lax.broadcasted_iota(jnp.int32, (columns, slabs), 0)
    for k in range(slots):
        marks = jnp.where(index[k : k + 1, :] == spots_down, 1.0, 0.0)
        onehot[:, k * slabs : (k + 1) * slabs] = marks.astype(jnp.bfloat16)
    live[...] = jnp.dot(
        onehot[...], jnp.ones((slabs * slots, width_z), jnp.bfloat16), preferred_element_type=jnp.float32)

    lane = lax.broadcasted_iota(jnp.int32, (ROWS, width_z), 1)
    row = lax.broadcasted_iota(jnp.int32, (ROWS, width_z), 0)
    cell_ids = row * width_z + lane
    not_last = lane < width_z - 1
    not_first = lane > 0
    plane = width_y * width_z
    loads[5].wait()
    loads[6].wait()
    source_cell = [ports_ref[sim, port] - me * (width_x * plane) for sim in range(2)]

    def next_z(values):
        return jnp.where(not_last, pltpu.roll(values, width_z - 1, 1), 0.0)

    def prev_z(values):
        return jnp.where(not_first, pltpu.roll(values, 1, 1), 0.0)

    def magnetic_rows(step, sim, layer, lo, rows):
        for y in range(lo, lo + rows, ROWS):
            at, nxt, hat = pl.ds(y, ROWS), pl.ds(y + 1, ROWS), pl.ds(PAD + y, ROWS)
            ex = elec[sim, 0, layer, at]
            ey = elec[sim, 1, layer, at]
            ez = elec[sim, 2, layer, at]
            if layer < last:
                ey_up, ez_up = elec[sim, 1, layer + 1, at], elec[sim, 2, layer + 1, at]
            else:
                ey_up, ez_up = face_up[step, sim, 0, at], face_up[step, sim, 1, at]
            magn[sim, 0, layer, hat] = magn[sim, 0, layer, hat] - magnetic_coef * (
                elec[sim, 2, layer, nxt] - ez - (next_z(ey) - ey))
            magn[sim, 1, layer, hat] = magn[sim, 1, layer, hat] - magnetic_coef * (
                next_z(ex) - ex - (ez_up - ez))
            magn[sim, 2, layer, hat] = magn[sim, 2, layer, hat] - magnetic_coef * (
                ey_up - ey - (elec[sim, 0, layer, nxt] - ex))

    def partial_rows(sim, lo, rows):
        for y in range(lo, lo + rows, ROWS):
            at, nxt, hat = pl.ds(y, ROWS), pl.ds(y + 1, ROWS), pl.ds(PAD + y, ROWS)
            ex = elec[sim, 0, last, at]
            partial[sim, 0, at] = magn[sim, 1, last, hat] - magnetic_coef * (
                next_z(ex) - ex + elec[sim, 2, last, at])
            partial[sim, 1, at] = magn[sim, 2, last, hat] + magnetic_coef * (
                elec[sim, 1, last, at] + (elec[sim, 0, last, nxt] - ex))

    halo_coef = jnp.where(has_below, magnetic_coef, 0.0).astype(jnp.float32)

    def electric_rows(step, sim, layer, lo, rows):
        pulse = waves_ref[sim, 0, step]
        for y in range(lo, lo + rows, ROWS):
            at, hat, prv = pl.ds(y, ROWS), pl.ds(PAD + y, ROWS), pl.ds(PAD + y - 1, ROWS)
            hx = magn[sim, 0, layer, hat]
            hy = magn[sim, 1, layer, hat]
            hz = magn[sim, 2, layer, hat]
            ex = elec[sim, 0, layer, at]
            ey = elec[sim, 1, layer, at]
            ez = elec[sim, 2, layer, at]
            if layer > 0:
                hy_down, hz_down = magn[sim, 1, layer - 1, hat], magn[sim, 2, layer - 1, hat]
            else:
                hy_down = face_down[step, sim, 0, at] + halo_coef * ez
                hz_down = face_down[step, sim, 1, at] - halo_coef * ey
            cx = hz - magn[sim, 2, layer, prv] - (hy - prev_z(hy))
            cy = hx - prev_z(hx) - (hz - hz_down)
            cz = hy - hy_down - (hx - magn[sim, 0, layer, prv])
            xy, xz, yz = tensor[3, layer, at], tensor[4, layer, at], tensor[5, layer, at]
            ex = ex + (tensor[0, layer, at] * cx + xy * cy + xz * cz)
            ey = ey + (xy * cx + tensor[1, layer, at] * cy + yz * cz)
            ez = ez + (xz * cx + yz * cy + tensor[2, layer, at] * cz)
            here = source_cell[sim] - (layer * plane + y * width_z)
            ez = ez + jnp.where(cell_ids == here, pulse, 0.0)
            elec[sim, 0, layer, at] = ex
            elec[sim, 1, layer, at] = ey
            elec[sim, 2, layer, at] = ez
            if sim == 1:
                summed[layer, at] = summed[layer, at] + (
                    elec[0, 0, layer, at] * ex + elec[0, 1, layer, at] * ey + elec[0, 2, layer, at] * ez)

    loads[0].wait()
    loads[1].wait()
    for sim in range(2):
        partial_rows(sim, 0, width_y)

    pl.semaphore_wait(barrier, slabs - 1 + port_devices - 1)

    def first_faces(up_rows, down_rows):
        @pl.when(has_above)
        def _():
            for sim in range(2):
                for lo in pieces(up_rows):
                    up_copy(0, sim, lo, up_rows).start()

        @pl.when(has_below)
        def _():
            for sim in range(2):
                for lo in pieces(down_rows):
                    down_copy(
                        0, sim, lo, down_rows,
                        fields.at[sim, 0, pl.ds(1, 2), 0, pl.ds(lo, down_rows)]).start()

    by_side(lambda: first_faces(FAR_ROWS, width_y), lambda: first_faces(width_y, FAR_ROWS))

    for k in sorted(range(1, slabs), key=lambda k: abs(k - slabs / 2)):
        tile_copy(k).start()

    def magnetic_inside(sim):
        for layer in range(last):
            magnetic_rows(None, sim, layer, 0, width_y)

    for sim in range(2):
        magnetic_inside(sim)
    loads[2].wait()
    loads[4].wait()

    def take_tiles(k, carry):
        tile_copy(k).wait_recv()
        return carry

    def tiles_gone(k, carry):
        tile_copy(k).wait_send()
        return carry

    def place_tiles():
        for entry in range(6):
            block = jnp.concatenate(
                [arrived[pl.ds(6 * k + entry, slabs, stride=owner_rows), :] for k in range(slots)], 0)
            high = block.astype(jnp.bfloat16)
            rest = block - high.astype(jnp.float32)
            middle = rest.astype(jnp.bfloat16)
            low = (rest - middle.astype(jnp.float32)).astype(jnp.bfloat16)
            spots = onehot[...]
            placed = (
                jnp.dot(spots, low, preferred_element_type=jnp.float32)
                + jnp.dot(spots, middle, preferred_element_type=jnp.float32)
                + jnp.dot(spots, high, preferred_element_type=jnp.float32))
            for layer in range(width_x):
                part = placed[layer * width_y : (layer + 1) * width_y]
                taken = live[pl.ds(layer * width_y, width_y)] > 0.5
                tensor[entry, layer] = jnp.where(taken, part, bulk[entry, layer] if entry < 3 else 0.0)

    def share_span(device):
        return pl.ds(pl.multiple_of(device * share_rows, 8), share_rows)

    def share_copy(k, group, layers):
        target = lax.rem(port + k, port_devices)
        return pltpu.make_async_remote_copy(
            summed.at[layers, share_span(target)], shares.at[k, layers],
            share_send.at[k, group], share_recv.at[k, group], device_id=(me, target), device_id_type=MESH)

    def share_out(step, sim, group, layers):
        if sim == 1:
            @pl.when(step == steps - 1)
            def _():
                for k in range(1, port_devices):
                    share_copy(k, group, layers).start()

    def top_rows(step, sim, rows):
        def send(lo):
            @pl.when(jnp.logical_and(has_above, step < steps - 1))
            def _():
                up_copy(step, sim, lo, rows).wait_send()
                partial_rows(sim, lo, rows)
                up_copy(step + 1, sim, lo, rows).start()

        for lo in pieces(rows):
            @pl.when(has_above)
            def _():
                down_copy(step, sim, lo, rows).wait_recv()
            magnetic_rows(step, sim, last, lo, rows)
            electric_rows(step, sim, last, lo, rows)
            if lo > 0:
                send(lo - rows)
        send(width_y - rows)

    def bottom_rows(step, sim, rows):
        for lo in pieces(rows):
            @pl.when(has_below)
            def _():
                up_copy(step, sim, lo, rows).wait_recv()
                down_copy(step, sim, lo, rows).wait_send()
            electric_rows(step, sim, 0, lo, rows)

            @pl.when(jnp.logical_and(has_below, step < steps - 1))
            def _():
                down_copy(step + 1, sim, lo, rows).start()

    lax.fori_loop(1, slabs, take_tiles, 0)
    place_tiles()

    def one_step(step, carry):
        for sim in range(2):
            for layer in range(1, last):
                electric_rows(step, sim, layer, 0, width_y)

            def odd():
                bottom_rows(step, sim, width_y)
                share_out(step, sim, 0, pl.ds(0, last))
                top_rows(step, sim, FAR_ROWS)
                share_out(step, sim, 1, pl.ds(last, 1))

            def even():
                top_rows(step, sim, width_y)
                share_out(step, sim, 0, pl.ds(1, last))
                bottom_rows(step, sim, FAR_ROWS)
                share_out(step, sim, 1, pl.ds(0, 1))

            by_side(odd, even)

            @pl.when(step < steps - 1)
            def _():
                magnetic_inside(sim)
        return carry

    lax.fori_loop(0, steps, one_step, 0)

    def faces_gone(up_rows):
        @pl.when(has_above)
        def _():
            for sim in range(2):
                for lo in pieces(up_rows):
                    up_copy(0, sim, lo, up_rows).wait_send()

    by_side(lambda: faces_gone(FAR_ROWS), lambda: faces_gone(width_y))
    lax.fori_loop(1, slabs, tiles_gone, 0)

    def add_shares(parts):
        for k in range(1, port_devices):
            for group, layers in enumerate(parts):
                share_copy(k, group, layers).wait_recv()
        total = summed[:, share_span(port)]
        for k in range(1, port_devices):
            total = total + shares[k]
        result[...] = total * (1.0 / math.sqrt(ports_ref.shape[1] * steps))
        for k in range(1, port_devices):
            for group, layers in enumerate(parts):
                share_copy(k, group, layers).wait_send()

    by_side(
        lambda: add_shares((pl.ds(0, last), pl.ds(last, 1))),
        lambda: add_shares((pl.ds(1, last), pl.ds(0, 1))))


def store_kernel(elec, magn, total, out_fields, out_sens, sem):
    rows = out_fields.shape[4]
    copies = [
        pltpu.make_async_copy(elec.at[:, :, :, pl.ds(0, rows)], out_fields.at[:, 0, pl.ds(0, 3)], sem.at[0]),
        pltpu.make_async_copy(magn.at[:, :, :, pl.ds(PAD, rows)], out_fields.at[:, 0, pl.ds(3, 3)], sem.at[1]),
        pltpu.make_async_copy(total, out_sens, sem.at[2]),
    ]
    for copy in copies:
        copy.start()
    for copy in copies:
        copy.wait()


def solution(mesh):
    slabs, port_devices = mesh.shape["space"], mesh.shape["port"]

    def local(fields, inv_eps, tensor_tiles, tile_index, ports, waves):
        assert fields.shape[1] == 1
        width_x, width_y, width_z = fields.shape[3:]
        steps = waves.shape[2]
        slots = tile_index.shape[2]
        owner_rows = tensor_tiles.shape[2]
        share_rows = width_y // port_devices
        far_pieces = width_y // FAR_ROWS
        f32 = jnp.float32
        dma = pltpu.SemaphoreType.DMA
        held = pl.BlockSpec(memory_space=pltpu.HBM)
        onchip = pl.BlockSpec(memory_space=pltpu.VMEM)
        anywhere = pl.BlockSpec(memory_space=pl.ANY)
        state = pl.pallas_call(
            functools.partial(kernel, slabs, port_devices),
            out_shape=(
                pltpu.VMEM((2, 3, width_x, width_y + PAD, width_z), f32),
                pltpu.VMEM((2, 3, width_x, width_y + PAD, width_z), f32),
                pltpu.VMEM((width_x, share_rows, width_z), f32),
            ),
            in_specs=[held] * 6,
            out_specs=(onchip, onchip, onchip),
            scratch_shapes=[
                pltpu.SMEM(ports.shape, jnp.int32),
                pltpu.SMEM(waves.shape, f32),
                pltpu.VMEM((steps, 2, 2, width_y, width_z), f32),
                pltpu.VMEM((steps, 2, 2, width_y, width_z), f32),
                pltpu.VMEM((2, 2, width_y, width_z), f32),
                pltpu.VMEM((6, width_x, width_y, width_z), f32),
                pltpu.VMEM((3, width_x, width_y, width_z), f32),
                pltpu.VMEM((slabs * owner_rows, width_z), f32),
                pltpu.VMEM((slots, slabs), jnp.int32),
                pltpu.VMEM((width_x * width_y, slabs * slots), jnp.bfloat16),
                pltpu.VMEM((width_x * width_y, width_z), f32),
                pltpu.VMEM((width_x, width_y, width_z), f32),
                pltpu.VMEM((port_devices, width_x, share_rows, width_z), f32),
                dma((7,)),
                dma((slabs,)),
                dma((slabs,)),
                dma((2, far_pieces)),
                dma((steps, 2, far_pieces)),
                dma((2, far_pieces)),
                dma((steps, 2, far_pieces)),
                dma((port_devices, 2)),
                dma((port_devices, 2)),
            ],
            compiler_params=pltpu.CompilerParams(
                collective_id=0, has_side_effects=True, vmem_limit_bytes=40 * 1024 * 1024),
            name="window",
        )(*[pltpu.with_memory_space_constraint(x, pltpu.HBM) for x in (ports, waves, fields, inv_eps, tensor_tiles, tile_index.transpose(0, 2, 1))])
        return pl.pallas_call(
            store_kernel,
            out_shape=(
                jax.ShapeDtypeStruct(fields.shape, f32),
                jax.ShapeDtypeStruct((width_x, share_rows, width_z), f32),
            ),
            in_specs=[anywhere] * 3,
            out_specs=(anywhere, anywhere),
            scratch_shapes=[dma((3,))],
            compiler_params=pltpu.CompilerParams(vmem_limit_bytes=4 * 1024 * 1024),
            name="store",
        )(*[pltpu.with_memory_space_constraint(x, pltpu.VMEM) for x in state])

    in_specs = (
        P(None, "port", None, "space", None, None),
        P(None, "space", None, None),
        P("space", None, None, None),
        P("space", None, None),
        P(),
        P(None, "port", None),
    )
    out_specs = (P(None, "port", None, "space", None, None), P("space", "port", None))
    return jax.shard_map(local, mesh=mesh, in_specs=in_specs, out_specs=out_specs, check_vma=False)
```

```python
import functools
import math

import jax
import jax.numpy as jnp
from jax import lax
from jax.experimental import pallas as pl
from jax.experimental.pallas import tpu as pltpu
from jax.sharding import PartitionSpec as P

MESH = pl.DeviceIdType.MESH
magnetic_coef = 0.5
PAD = 8
ROWS = 16
FAR_ROWS = 16


def kernel(
    slabs, port_devices, ports_in, waves_in, fields, inv_eps, tiles, tile_index,
    elec, magn, result,
    ports_ref, waves_ref, face_up, face_down, partial, sending, pieces_ref, tensor, bulk, arrived, index, onehot, live, summed,
    shares, load_sem, tile_send, tile_recv, up_send, up_recv, down_send, down_recv,
    share_send, share_recv,
):
    me = lax.axis_index("space")
    port = lax.axis_index("port")
    width_x, width_y, width_z = inv_eps.shape[1:]
    steps = waves_ref.shape[2]
    last = width_x - 1
    owner_rows = tiles.shape[2]
    slots = owner_rows // 6
    share_rows = width_y // port_devices
    has_below = me > 0
    has_above = me < slabs - 1
    above = jnp.minimum(me + 1, slabs - 1)
    below = jnp.maximum(me - 1, 0)

    def owner_span(owner):
        return pl.ds(pl.multiple_of(owner * owner_rows, 8), owner_rows)

    barrier = pltpu.get_barrier_semaphore()

    far_first = sorted(range(1, slabs), key=lambda k: abs(k - slabs / 2))
    for k in far_first:
        pl.semaphore_signal(barrier, inc=1, device_id=(lax.rem(me + k, slabs), port), device_id_type=MESH)
    for k in range(1, port_devices):
        pl.semaphore_signal(
            barrier, inc=1, device_id=(me, lax.rem(port + k, port_devices)), device_id_type=MESH)


    loads = [
        pltpu.make_async_copy(fields.at[:, 0, pl.ds(0, 3)], elec.at[:, :, :, pl.ds(0, width_y)], load_sem.at[0]),
        pltpu.make_async_copy(fields.at[:, 0, pl.ds(3, 3)], magn.at[:, :, :, pl.ds(PAD, width_y)], load_sem.at[1]),
        pltpu.make_async_copy(inv_eps, bulk, load_sem.at[2]),
        pltpu.make_async_copy(tile_index.at[0], index, load_sem.at[3]),
        pltpu.make_async_copy(tiles.at[0, me], arrived.at[owner_span(me)], load_sem.at[4]),
        pltpu.make_async_copy(ports_in, ports_ref, load_sem.at[5]),
        pltpu.make_async_copy(waves_in, waves_ref, load_sem.at[6]),
        pltpu.make_async_copy(tiles.at[0], sending, load_sem.at[7]),
    ]
    for load in (loads[3], loads[5], loads[6], loads[0], loads[1], loads[7], loads[2], loads[4]):
        load.start()

    def up_copy(step, sim, lo, rows):
        span, k = pl.ds(lo, rows), lo // rows
        return pltpu.make_async_remote_copy(
            partial.at[sim, :, span], face_down.at[step, sim, :, span],
            up_send.at[sim, k], up_recv.at[step, sim, k], device_id=(above, port), device_id_type=MESH)

    def down_copy(step, sim, lo, rows):
        span, k = pl.ds(lo, rows), lo // rows
        return pltpu.make_async_remote_copy(
            elec.at[sim, pl.ds(1, 2), 0, span], face_up.at[step, sim, :, span],
            down_send.at[sim, k], down_recv.at[step, sim, k], device_id=(below, port), device_id_type=MESH)

    top_is_far = lax.rem(me, 2) == 1

    def by_side(odd, even):
        pl.when(top_is_far)(odd)
        pl.when(jnp.logical_not(top_is_far))(even)

    def pieces(rows):
        return range(0, width_y, rows)

    def tile_copy(k):
        target = lax.rem(me + k, slabs)
        return pltpu.make_async_remote_copy(
            sending.at[target], arrived.at[owner_span(me)],
            tile_send.at[k], tile_recv.at[k], device_id=(target, port), device_id_type=MESH)

    zero_rows = jnp.zeros((PAD, width_z), jnp.float32)
    for sim in range(2):
        for comp in range(3):
            for layer in range(width_x):
                elec[sim, comp, layer, pl.ds(width_y, PAD)] = zero_rows
                magn[sim, comp, layer, pl.ds(0, PAD)] = zero_rows
    zero_plane = jnp.zeros((width_y, width_z), jnp.float32)

    @pl.when(me == 0)
    def _():
        def clear(step, carry):
            for sim in range(2):
                for comp in range(2):
                    face_down[step, sim, comp] = zero_plane
            return carry
        lax.fori_loop(0, steps, clear, 0)

    @pl.when(me == slabs - 1)
    def _():
        def clear(step, carry):
            for sim in range(2):
                for comp in range(2):
                    face_up[step, sim, comp] = zero_plane
            return carry
        lax.fori_loop(0, steps, clear, 0)

    for layer in range(width_x):
        summed[layer] = zero_plane

    columns = width_x * width_y
    loads[3].wait()
    spots_down = lax.broadcasted_iota(jnp.int32, (columns, slabs), 0)
    for k in range(slots):
        marks = jnp.where(index[k : k + 1, :] == spots_down, 1.0, 0.0)
        onehot[:, k * slabs : (k + 1) * slabs] = marks.astype(jnp.bfloat16)
    live[...] = jnp.dot(
        onehot[...], jnp.ones((slabs * slots, width_z), jnp.bfloat16), preferred_element_type=jnp.float32)

    lane = lax.broadcasted_iota(jnp.int32, (ROWS, width_z), 1)
    row = lax.broadcasted_iota(jnp.int32, (ROWS, width_z), 0)
    cell_ids = row * width_z + lane
    not_last = lane < width_z - 1
    not_first = lane > 0
    plane = width_y * width_z
    loads[5].wait()
    loads[6].wait()
    source_cell = [ports_ref[sim, port] - me * (width_x * plane) for sim in range(2)]

    def next_z(values):
        return jnp.where(not_last, pltpu.roll(values, width_z - 1, 1), 0.0)

    def prev_z(values):
        return jnp.where(not_first, pltpu.roll(values, 1, 1), 0.0)

    def magnetic_rows(step, sim, layer, lo, rows):
        for y in range(lo, lo + rows, ROWS):
            at, nxt, hat = pl.ds(y, ROWS), pl.ds(y + 1, ROWS), pl.ds(PAD + y, ROWS)
            ex = elec[sim, 0, layer, at]
            ey = elec[sim, 1, layer, at]
            ez = elec[sim, 2, layer, at]
            if layer < last:
                ey_up, ez_up = elec[sim, 1, layer + 1, at], elec[sim, 2, layer + 1, at]
            else:
                ey_up, ez_up = face_up[step, sim, 0, at], face_up[step, sim, 1, at]
            magn[sim, 0, layer, hat] = magn[sim, 0, layer, hat] - magnetic_coef * (
                elec[sim, 2, layer, nxt] - ez - (next_z(ey) - ey))
            magn[sim, 1, layer, hat] = magn[sim, 1, layer, hat] - magnetic_coef * (
                next_z(ex) - ex - (ez_up - ez))
            magn[sim, 2, layer, hat] = magn[sim, 2, layer, hat] - magnetic_coef * (
                ey_up - ey - (elec[sim, 0, layer, nxt] - ex))

    def partial_rows(sim, lo, rows):
        for y in range(lo, lo + rows, ROWS):
            at, nxt, hat = pl.ds(y, ROWS), pl.ds(y + 1, ROWS), pl.ds(PAD + y, ROWS)
            ex = elec[sim, 0, last, at]
            partial[sim, 0, at] = magn[sim, 1, last, hat] - magnetic_coef * (
                next_z(ex) - ex + elec[sim, 2, last, at])
            partial[sim, 1, at] = magn[sim, 2, last, hat] + magnetic_coef * (
                elec[sim, 1, last, at] + (elec[sim, 0, last, nxt] - ex))

    halo_coef = jnp.where(has_below, magnetic_coef, 0.0).astype(jnp.float32)

    def electric_rows(step, sim, layer, lo, rows):
        pulse = waves_ref[sim, 0, step]
        for y in range(lo, lo + rows, ROWS):
            at, hat, prv = pl.ds(y, ROWS), pl.ds(PAD + y, ROWS), pl.ds(PAD + y - 1, ROWS)
            hx = magn[sim, 0, layer, hat]
            hy = magn[sim, 1, layer, hat]
            hz = magn[sim, 2, layer, hat]
            ex = elec[sim, 0, layer, at]
            ey = elec[sim, 1, layer, at]
            ez = elec[sim, 2, layer, at]
            if layer > 0:
                hy_down, hz_down = magn[sim, 1, layer - 1, hat], magn[sim, 2, layer - 1, hat]
            else:
                hy_down = face_down[step, sim, 0, at] + halo_coef * ez
                hz_down = face_down[step, sim, 1, at] - halo_coef * ey
            cx = hz - magn[sim, 2, layer, prv] - (hy - prev_z(hy))
            cy = hx - prev_z(hx) - (hz - hz_down)
            cz = hy - hy_down - (hx - magn[sim, 0, layer, prv])
            xy, xz, yz = tensor[3, layer, at], tensor[4, layer, at], tensor[5, layer, at]
            ex = ex + (tensor[0, layer, at] * cx + xy * cy + xz * cz)
            ey = ey + (xy * cx + tensor[1, layer, at] * cy + yz * cz)
            ez = ez + (xz * cx + yz * cy + tensor[2, layer, at] * cz)
            here = source_cell[sim] - (layer * plane + y * width_z)
            ez = ez + jnp.where(cell_ids == here, pulse, 0.0)
            elec[sim, 0, layer, at] = ex
            elec[sim, 1, layer, at] = ey
            elec[sim, 2, layer, at] = ez
            if sim == 1:
                summed[layer, at] = summed[layer, at] + (
                    elec[0, 0, layer, at] * ex + elec[0, 1, layer, at] * ey + elec[0, 2, layer, at] * ez)

    loads[0].wait()
    loads[1].wait()
    for sim in range(2):
        partial_rows(sim, 0, width_y)

    loads[7].wait()
    pl.semaphore_wait(barrier, slabs - 1 + port_devices - 1)

    for k in far_first:
        tile_copy(k).start()

    def first_faces(up_rows, down_rows):
        @pl.when(has_above)
        def _():
            for sim in range(2):
                for lo in pieces(up_rows):
                    up_copy(0, sim, lo, up_rows).start()

        @pl.when(has_below)
        def _():
            for sim in range(2):
                for lo in pieces(down_rows):
                    down_copy(0, sim, lo, down_rows).start()

    by_side(lambda: first_faces(FAR_ROWS, width_y), lambda: first_faces(width_y, FAR_ROWS))

    def magnetic_inside(sim):
        for layer in range(last):
            magnetic_rows(None, sim, layer, 0, width_y)

    for sim in range(2):
        magnetic_inside(sim)
    loads[2].wait()
    loads[4].wait()

    def take_tiles(k, carry):
        tile_copy(k).wait_recv()
        return carry

    def tiles_gone(k, carry):
        tile_copy(k).wait_send()
        return carry

    def split_tiles():
        for entry in range(6):
            block = jnp.concatenate(
                [arrived[pl.ds(6 * k + entry, slabs, stride=owner_rows), :] for k in range(slots)], 0)
            high = block.astype(jnp.bfloat16)
            rest = block - high.astype(jnp.float32)
            middle = rest.astype(jnp.bfloat16)
            pieces_ref[entry, 0] = high
            pieces_ref[entry, 1] = middle
            pieces_ref[entry, 2] = (rest - middle.astype(jnp.float32)).astype(jnp.bfloat16)

    def place_tiles(layer):
        rows = pl.ds(pl.multiple_of(layer * width_y, 16), width_y)
        spots = onehot[rows, :]
        taken = live[rows, :] > 0.5
        for entry in range(6):
            placed = (
                jnp.dot(spots, pieces_ref[entry, 2], preferred_element_type=jnp.float32)
                + jnp.dot(spots, pieces_ref[entry, 1], preferred_element_type=jnp.float32)
                + jnp.dot(spots, pieces_ref[entry, 0], preferred_element_type=jnp.float32))
            tensor[entry, layer] = jnp.where(taken, placed, bulk[entry, layer] if entry < 3 else 0.0)

    def place_rest(k, carry):
        place_tiles(k + jnp.where(top_is_far, 0, 1))
        return carry

    def share_span(device):
        return pl.ds(pl.multiple_of(device * share_rows, 8), share_rows)

    def share_copy(k, group, layers):
        target = lax.rem(port + k, port_devices)
        return pltpu.make_async_remote_copy(
            summed.at[layers, share_span(target)], shares.at[k, layers],
            share_send.at[k, group], share_recv.at[k, group], device_id=(me, target), device_id_type=MESH)

    def share_out(step, sim, group, layers):
        if sim == 1:
            @pl.when(step == steps - 1)
            def _():
                for k in range(1, port_devices):
                    share_copy(k, group, layers).start()

    def top_rows(step, sim, rows):
        def send(lo):
            @pl.when(jnp.logical_and(has_above, step < steps - 1))
            def _():
                up_copy(step, sim, lo, rows).wait_send()
                partial_rows(sim, lo, rows)
                up_copy(step + 1, sim, lo, rows).start()

        for lo in pieces(rows):
            @pl.when(has_above)
            def _():
                down_copy(step, sim, lo, rows).wait_recv()
            magnetic_rows(step, sim, last, lo, rows)
            electric_rows(step, sim, last, lo, rows)
            if lo > 0:
                send(lo - rows)
        send(width_y - rows)

    def bottom_rows(step, sim, rows):
        for lo in pieces(rows):
            @pl.when(has_below)
            def _():
                up_copy(step, sim, lo, rows).wait_recv()
                down_copy(step, sim, lo, rows).wait_send()
            electric_rows(step, sim, 0, lo, rows)

            @pl.when(jnp.logical_and(has_below, step < steps - 1))
            def _():
                down_copy(step + 1, sim, lo, rows).start()

    lax.fori_loop(1, slabs, take_tiles, 0)
    split_tiles()
    place_tiles(jnp.where(top_is_far, last, 0))

    def one_step(step, carry):
        for sim in range(2):
            def far_side():
                def odd():
                    top_rows(step, sim, FAR_ROWS)
                    share_out(step, sim, 1, pl.ds(last, 1))

                def even():
                    bottom_rows(step, sim, FAR_ROWS)
                    share_out(step, sim, 1, pl.ds(0, 1))

                by_side(odd, even)

            def near_side():
                if sim == 0:
                    @pl.when(step == 0)
                    def _():
                        lax.fori_loop(0, last, place_rest, 0)
                for layer in range(1, last):
                    electric_rows(step, sim, layer, 0, width_y)

                def odd():
                    bottom_rows(step, sim, width_y)
                    share_out(step, sim, 0, pl.ds(0, last))

                def even():
                    top_rows(step, sim, width_y)
                    share_out(step, sim, 0, pl.ds(1, last))

                by_side(odd, even)

            def one_side(turn, carry):
                far_turn = turn == jnp.where(step == 0, 0, 1)
                pl.when(far_turn)(far_side)
                pl.when(jnp.logical_not(far_turn))(near_side)
                return carry

            lax.fori_loop(0, 2, one_side, 0)

            @pl.when(step < steps - 1)
            def _():
                magnetic_inside(sim)
        return carry

    lax.fori_loop(0, steps, one_step, 0)

    def faces_gone(up_rows):
        @pl.when(has_above)
        def _():
            for sim in range(2):
                for lo in pieces(up_rows):
                    up_copy(0, sim, lo, up_rows).wait_send()

    by_side(lambda: faces_gone(FAR_ROWS), lambda: faces_gone(width_y))
    lax.fori_loop(1, slabs, tiles_gone, 0)

    def add_shares(parts):
        for k in range(1, port_devices):
            for group, layers in enumerate(parts):
                share_copy(k, group, layers).wait_recv()
        total = summed[:, share_span(port)]
        for k in range(1, port_devices):
            total = total + shares[k]
        result[...] = total * (1.0 / math.sqrt(ports_ref.shape[1] * steps))
        for k in range(1, port_devices):
            for group, layers in enumerate(parts):
                share_copy(k, group, layers).wait_send()

    by_side(
        lambda: add_shares((pl.ds(0, last), pl.ds(last, 1))),
        lambda: add_shares((pl.ds(1, last), pl.ds(0, 1))))


def store_kernel(elec, magn, total, out_fields, out_sens, sem):
    rows = out_fields.shape[4]
    copies = [pltpu.make_async_copy(total, out_sens, sem.at[0])]
    for sim in range(2):
        for comp in range(3):
            copies.append(pltpu.make_async_copy(
                elec.at[sim, comp, :, pl.ds(0, rows)], out_fields.at[sim, 0, comp], sem.at[len(copies)]))
            copies.append(pltpu.make_async_copy(
                magn.at[sim, comp, :, pl.ds(PAD, rows)], out_fields.at[sim, 0, 3 + comp], sem.at[len(copies)]))
    for copy in copies:
        copy.start()
    for copy in copies:
        copy.wait()


def solution(mesh):
    slabs, port_devices = mesh.shape["space"], mesh.shape["port"]

    def local(fields, inv_eps, tensor_tiles, tile_index, ports, waves):
        assert fields.shape[1] == 1
        width_x, width_y, width_z = fields.shape[3:]
        steps = waves.shape[2]
        slots = tile_index.shape[2]
        owner_rows = tensor_tiles.shape[2]
        share_rows = width_y // port_devices
        far_pieces = width_y // FAR_ROWS
        f32 = jnp.float32
        dma = pltpu.SemaphoreType.DMA
        held = pl.BlockSpec(memory_space=pltpu.HBM)
        onchip = pl.BlockSpec(memory_space=pltpu.VMEM)
        anywhere = pl.BlockSpec(memory_space=pl.ANY)
        state = pl.pallas_call(
            functools.partial(kernel, slabs, port_devices),
            out_shape=(
                pltpu.VMEM((2, 3, width_x, width_y + PAD, width_z), f32),
                pltpu.VMEM((2, 3, width_x, width_y + PAD, width_z), f32),
                pltpu.VMEM((width_x, share_rows, width_z), f32),
            ),
            in_specs=[held] * 6,
            out_specs=(onchip, onchip, onchip),
            scratch_shapes=[
                pltpu.SMEM(ports.shape, jnp.int32),
                pltpu.SMEM(waves.shape, f32),
                pltpu.VMEM((steps, 2, 2, width_y, width_z), f32),
                pltpu.VMEM((steps, 2, 2, width_y, width_z), f32),
                pltpu.VMEM((2, 2, width_y, width_z), f32),
                pltpu.VMEM((slabs, owner_rows, width_z), f32),
                pltpu.VMEM((6, 3, slabs * slots, width_z), jnp.bfloat16),
                pltpu.VMEM((6, width_x, width_y, width_z), f32),
                pltpu.VMEM((3, width_x, width_y, width_z), f32),
                pltpu.VMEM((slabs * owner_rows, width_z), f32),
                pltpu.VMEM((slots, slabs), jnp.int32),
                pltpu.VMEM((width_x * width_y, slabs * slots), jnp.bfloat16),
                pltpu.VMEM((width_x * width_y, width_z), f32),
                pltpu.VMEM((width_x, width_y, width_z), f32),
                pltpu.VMEM((port_devices, width_x, share_rows, width_z), f32),
                dma((8,)),
                dma((slabs,)),
                dma((slabs,)),
                dma((2, far_pieces)),
                dma((steps, 2, far_pieces)),
                dma((2, far_pieces)),
                dma((steps, 2, far_pieces)),
                dma((port_devices, 2)),
                dma((port_devices, 2)),
            ],
            compiler_params=pltpu.CompilerParams(
                collective_id=0, has_side_effects=True, vmem_limit_bytes=40 * 1024 * 1024),
            name="window",
        )(*[pltpu.with_memory_space_constraint(x, pltpu.HBM) for x in (ports, waves, fields, inv_eps, tensor_tiles, tile_index.transpose(0, 2, 1))])
        return pl.pallas_call(
            store_kernel,
            out_shape=(
                jax.ShapeDtypeStruct(fields.shape, f32),
                jax.ShapeDtypeStruct((width_x, share_rows, width_z), f32),
            ),
            in_specs=[anywhere] * 3,
            out_specs=(anywhere, anywhere),
            scratch_shapes=[dma((13,))],
            compiler_params=pltpu.CompilerParams(vmem_limit_bytes=4 * 1024 * 1024),
            name="store",
        )(*[pltpu.with_memory_space_constraint(x, pltpu.VMEM) for x in state])

    in_specs = (
        P(None, "port", None, "space", None, None),
        P(None, "space", None, None),
        P("space", None, None, None),
        P("space", None, None),
        P(),
        P(None, "port", None),
    )
    out_specs = (P(None, "port", None, "space", None, None), P("space", "port", None))
    return jax.shard_map(local, mesh=mesh, in_specs=in_specs, out_specs=out_specs, check_vma=False)
```

```python
import functools
import math

import jax
import jax.numpy as jnp
from jax import lax
from jax.experimental import pallas as pl
from jax.experimental.pallas import tpu as pltpu
from jax.sharding import PartitionSpec as P

MESH = pl.DeviceIdType.MESH
magnetic_coef = 0.5
PAD = 8
ROWS = 16
FAR_ROWS = 16
GROUPS = 4


def kernel(
    slabs, port_devices, ports_in, waves_in, fields, inv_eps, tiles, tile_index,
    elec, magn, result,
    ports_ref, waves_ref, face_up, face_down, partial, pieces_ref, tensor, bulk, arrived, index, onehot, live, summed,
    shares, load_sem, tile_send, tile_recv, up_send, up_recv, down_send, down_recv,
    share_send, share_recv, ready, port_ready,
):
    me = lax.axis_index("space")
    port = lax.axis_index("port")
    width_x, width_y, width_z = inv_eps.shape[1:]
    steps = waves_ref.shape[2]
    last = width_x - 1
    owner_rows = tiles.shape[2]
    slots = owner_rows // 6
    share_rows = width_y // port_devices
    has_below = me > 0
    has_above = me < slabs - 1
    above = jnp.minimum(me + 1, slabs - 1)
    below = jnp.maximum(me - 1, 0)

    def owner_span(owner):
        return pl.ds(pl.multiple_of(owner * owner_rows, 8), owner_rows)

    barrier = pltpu.get_barrier_semaphore()

    size = slabs // GROUPS
    group = me // size

    def signal(semaphore, slab, along):
        pl.semaphore_signal(semaphore, inc=1, device_id=(slab, along), device_id_type=MESH)

    def await_all(semaphore, count):
        @pl.when(count > 0)
        def _():
            pl.semaphore_wait(semaphore, count)

    def each(low, high, act):
        def body(slab, carry):
            act(slab)
            return carry
        lax.fori_loop(low, high, body, 0)

    each(me + 1, slabs, lambda slab: signal(barrier, slab, port))
    each(port + 1, port_devices, lambda along: signal(barrier, me, along))

    loads = [
        pltpu.make_async_copy(fields.at[:, 0, pl.ds(0, 3)], elec.at[:, :, :, pl.ds(0, width_y)], load_sem.at[0]),
        pltpu.make_async_copy(fields.at[:, 0, pl.ds(3, 3)], magn.at[:, :, :, pl.ds(PAD, width_y)], load_sem.at[1]),
        pltpu.make_async_copy(inv_eps, bulk, load_sem.at[2]),
        pltpu.make_async_copy(tile_index.at[0], index, load_sem.at[3]),
        pltpu.make_async_copy(tiles.at[0, me], arrived.at[owner_span(me)], load_sem.at[4]),
        pltpu.make_async_copy(ports_in, ports_ref, load_sem.at[5]),
        pltpu.make_async_copy(waves_in, waves_ref, load_sem.at[6]),
    ]
    for load in (loads[3], loads[5], loads[6], loads[0], loads[1], loads[2], loads[4]):
        load.start()

    def up_copy(step, sim, lo, rows):
        span, k = pl.ds(lo, rows), lo // rows
        return pltpu.make_async_remote_copy(
            partial.at[sim, :, span], face_down.at[step, sim, :, span],
            up_send.at[sim, k], up_recv.at[step, sim, k], device_id=(above, port), device_id_type=MESH)

    def down_copy(step, sim, lo, rows):
        span, k = pl.ds(lo, rows), lo // rows
        return pltpu.make_async_remote_copy(
            elec.at[sim, pl.ds(1, 2), 0, span], face_up.at[step, sim, :, span],
            down_send.at[sim, k], down_recv.at[step, sim, k], device_id=(below, port), device_id_type=MESH)

    top_is_far = lax.rem(me, 2) == 1

    def by_side(odd, even):
        pl.when(top_is_far)(odd)
        pl.when(jnp.logical_not(top_is_far))(even)

    def pieces(rows):
        return range(0, width_y, rows)

    def tile_copy(k):
        target = lax.rem(me + k, slabs)
        return pltpu.make_async_remote_copy(
            tiles.at[0, target], arrived.at[owner_span(me)],
            tile_send.at[k], tile_recv.at[k], device_id=(target, port), device_id_type=MESH)

    def send_tile(slab):
        tile_copy(lax.rem(slab - me + slabs, slabs)).start()

    await_all(barrier, me + port)
    each(0, me, lambda slab: signal(ready.at[group - slab // size], slab, port))
    each(0, port, lambda along: signal(port_ready, me, along))
    each(0, me, send_tile)

    for offset in range(1):
        ahead = group + offset

        @pl.when(ahead < GROUPS)
        def _():
            low = jnp.maximum(ahead * size, me + 1)
            high = (ahead + 1) * size
            await_all(ready.at[offset], high - low)
            each(low, high, send_tile)

    zero_rows = jnp.zeros((PAD, width_z), jnp.float32)
    for sim in range(2):
        for comp in range(3):
            for layer in range(width_x):
                elec[sim, comp, layer, pl.ds(width_y, PAD)] = zero_rows
                magn[sim, comp, layer, pl.ds(0, PAD)] = zero_rows
    zero_plane = jnp.zeros((width_y, width_z), jnp.float32)

    @pl.when(me == 0)
    def _():
        def clear(step, carry):
            for sim in range(2):
                for comp in range(2):
                    face_down[step, sim, comp] = zero_plane
            return carry
        lax.fori_loop(0, steps, clear, 0)

    @pl.when(me == slabs - 1)
    def _():
        def clear(step, carry):
            for sim in range(2):
                for comp in range(2):
                    face_up[step, sim, comp] = zero_plane
            return carry
        lax.fori_loop(0, steps, clear, 0)

    for layer in range(width_x):
        summed[layer] = zero_plane

    columns = width_x * width_y
    loads[3].wait()
    spots_down = lax.broadcasted_iota(jnp.int32, (columns, slabs), 0)
    for k in range(slots):
        marks = jnp.where(index[k : k + 1, :] == spots_down, 1.0, 0.0).astype(jnp.bfloat16)
        for part in range(3):
            onehot[:, (part * slots + k) * slabs : (part * slots + k + 1) * slabs] = marks
    live[...] = jnp.dot(
        onehot[...], jnp.ones((3 * slabs * slots, width_z), jnp.bfloat16), preferred_element_type=jnp.float32)

    lane = lax.broadcasted_iota(jnp.int32, (ROWS, width_z), 1)
    row = lax.broadcasted_iota(jnp.int32, (ROWS, width_z), 0)
    cell_ids = row * width_z + lane
    not_last = lane < width_z - 1
    not_first = lane > 0
    plane = width_y * width_z
    loads[5].wait()
    loads[6].wait()
    source_cell = [ports_ref[sim, port] - me * (width_x * plane) for sim in range(2)]

    def next_z(values):
        return jnp.where(not_last, pltpu.roll(values, width_z - 1, 1), 0.0)

    def prev_z(values):
        return jnp.where(not_first, pltpu.roll(values, 1, 1), 0.0)

    def magnetic_rows(step, sim, layer, lo, rows):
        for y in range(lo, lo + rows, ROWS):
            at, nxt, hat = pl.ds(y, ROWS), pl.ds(y + 1, ROWS), pl.ds(PAD + y, ROWS)
            ex = elec[sim, 0, layer, at]
            ey = elec[sim, 1, layer, at]
            ez = elec[sim, 2, layer, at]
            if layer < last:
                ey_up, ez_up = elec[sim, 1, layer + 1, at], elec[sim, 2, layer + 1, at]
            else:
                ey_up, ez_up = face_up[step, sim, 0, at], face_up[step, sim, 1, at]
            magn[sim, 0, layer, hat] = magn[sim, 0, layer, hat] - magnetic_coef * (
                elec[sim, 2, layer, nxt] - ez - (next_z(ey) - ey))
            magn[sim, 1, layer, hat] = magn[sim, 1, layer, hat] - magnetic_coef * (
                next_z(ex) - ex - (ez_up - ez))
            magn[sim, 2, layer, hat] = magn[sim, 2, layer, hat] - magnetic_coef * (
                ey_up - ey - (elec[sim, 0, layer, nxt] - ex))

    def partial_rows(sim, lo, rows):
        for y in range(lo, lo + rows, ROWS):
            at, nxt, hat = pl.ds(y, ROWS), pl.ds(y + 1, ROWS), pl.ds(PAD + y, ROWS)
            ex = elec[sim, 0, last, at]
            partial[sim, 0, at] = magn[sim, 1, last, hat] - magnetic_coef * (
                next_z(ex) - ex + elec[sim, 2, last, at])
            partial[sim, 1, at] = magn[sim, 2, last, hat] + magnetic_coef * (
                elec[sim, 1, last, at] + (elec[sim, 0, last, nxt] - ex))

    halo_coef = jnp.where(has_below, magnetic_coef, 0.0).astype(jnp.float32)

    def electric_rows(step, sim, layer, lo, rows):
        pulse = waves_ref[sim, 0, step]
        for y in range(lo, lo + rows, ROWS):
            at, hat, prv = pl.ds(y, ROWS), pl.ds(PAD + y, ROWS), pl.ds(PAD + y - 1, ROWS)
            hx = magn[sim, 0, layer, hat]
            hy = magn[sim, 1, layer, hat]
            hz = magn[sim, 2, layer, hat]
            ex = elec[sim, 0, layer, at]
            ey = elec[sim, 1, layer, at]
            ez = elec[sim, 2, layer, at]
            if layer > 0:
                hy_down, hz_down = magn[sim, 1, layer - 1, hat], magn[sim, 2, layer - 1, hat]
            else:
                hy_down = face_down[step, sim, 0, at] + halo_coef * ez
                hz_down = face_down[step, sim, 1, at] - halo_coef * ey
            cx = hz - magn[sim, 2, layer, prv] - (hy - prev_z(hy))
            cy = hx - prev_z(hx) - (hz - hz_down)
            cz = hy - hy_down - (hx - magn[sim, 0, layer, prv])
            xy, xz, yz = tensor[3, layer, at], tensor[4, layer, at], tensor[5, layer, at]
            ex = ex + (tensor[0, layer, at] * cx + xy * cy + xz * cz)
            ey = ey + (xy * cx + tensor[1, layer, at] * cy + yz * cz)
            ez = ez + (xz * cx + yz * cy + tensor[2, layer, at] * cz)
            here = source_cell[sim] - (layer * plane + y * width_z)
            ez = ez + jnp.where(cell_ids == here, pulse, 0.0)
            elec[sim, 0, layer, at] = ex
            elec[sim, 1, layer, at] = ey
            elec[sim, 2, layer, at] = ez
            if sim == 1:
                summed[layer, at] = summed[layer, at] + (
                    elec[0, 0, layer, at] * ex + elec[0, 1, layer, at] * ey + elec[0, 2, layer, at] * ez)

    loads[0].wait()
    loads[1].wait()
    for sim in range(2):
        partial_rows(sim, 0, width_y)

    for offset in range(1, GROUPS):
        ahead = group + offset

        @pl.when(ahead < GROUPS)
        def _():
            low = jnp.maximum(ahead * size, me + 1)
            high = (ahead + 1) * size
            await_all(ready.at[offset], high - low)
            each(low, high, send_tile)

    def first_faces(up_rows, down_rows):
        @pl.when(has_above)
        def _():
            for sim in range(2):
                for lo in pieces(up_rows):
                    up_copy(0, sim, lo, up_rows).start()

        @pl.when(has_below)
        def _():
            for sim in range(2):
                for lo in pieces(down_rows):
                    down_copy(0, sim, lo, down_rows).start()

    by_side(lambda: first_faces(FAR_ROWS, width_y), lambda: first_faces(width_y, FAR_ROWS))

    def magnetic_inside(sim):
        for layer in range(last):
            magnetic_rows(None, sim, layer, 0, width_y)

    for sim in range(2):
        magnetic_inside(sim)
    loads[2].wait()
    loads[4].wait()

    def take_tiles(k, carry):
        tile_copy(k).wait_recv()
        return carry

    def tiles_gone(k, carry):
        tile_copy(k).wait_send()
        return carry

    def split_tiles():
        for entry in range(6):
            block = jnp.concatenate(
                [arrived[pl.ds(6 * k + entry, slabs, stride=owner_rows), :] for k in range(slots)], 0)
            high = block.astype(jnp.bfloat16)
            rest = block - high.astype(jnp.float32)
            middle = rest.astype(jnp.bfloat16)
            low = (rest - middle.astype(jnp.float32)).astype(jnp.bfloat16)
            for part, values in enumerate((high, middle, low)):
                pieces_ref[entry, part * slots * slabs : (part + 1) * slots * slabs] = values

    def place_tiles(layer):
        rows = pl.ds(pl.multiple_of(layer * width_y, 16), width_y)
        spots = onehot[rows, :]
        taken = live[rows, :] > 0.5
        for entry in range(6):
            placed = jnp.dot(spots, pieces_ref[entry], preferred_element_type=jnp.float32)
            tensor[entry, layer] = jnp.where(taken, placed, bulk[entry, layer] if entry < 3 else 0.0)

    def place_rest(k, carry):
        place_tiles(k + jnp.where(top_is_far, 0, 1))
        return carry

    def share_span(device):
        return pl.ds(pl.multiple_of(device * share_rows, 8), share_rows)

    def share_copy(k, group, layers):
        target = lax.rem(port + k, port_devices)
        return pltpu.make_async_remote_copy(
            summed.at[layers, share_span(target)], shares.at[k, layers],
            share_send.at[k, group], share_recv.at[k, group], device_id=(me, target), device_id_type=MESH)

    def share_out(step, sim, group, layers, lo, rows):
        if sim == 1:
            for k in range(1, port_devices):
                end = (lax.rem(port + k, port_devices) + 1) * share_rows

                @pl.when((step == steps - 1) & (end > lo) & (end <= lo + rows))
                def _():
                    share_copy(k, group, layers).start()

    def top_rows(step, sim, rows, far):
        def send(lo):
            @pl.when(jnp.logical_and(has_above, step < steps - 1))
            def _():
                up_copy(step, sim, lo, rows).wait_send()
                partial_rows(sim, lo, rows)
                up_copy(step + 1, sim, lo, rows).start()

        for lo in pieces(rows):
            @pl.when(has_above)
            def _():
                down_copy(step, sim, lo, rows).wait_recv()
            magnetic_rows(step, sim, last, lo, rows)
            electric_rows(step, sim, last, lo, rows)
            if far:
                share_out(step, sim, 1, pl.ds(last, 1), lo, rows)
            if lo > 0:
                send(lo - rows)
        send(width_y - rows)

    def bottom_rows(step, sim, rows, far):
        for lo in pieces(rows):
            @pl.when(has_below)
            def _():
                up_copy(step, sim, lo, rows).wait_recv()
                down_copy(step, sim, lo, rows).wait_send()
            electric_rows(step, sim, 0, lo, rows)
            if far:
                share_out(step, sim, 1, pl.ds(0, 1), lo, rows)

            @pl.when(jnp.logical_and(has_below, step < steps - 1))
            def _():
                down_copy(step + 1, sim, lo, rows).start()

    lax.fori_loop(1, slabs, take_tiles, 0)
    await_all(port_ready, port_devices - 1 - port)
    split_tiles()
    place_tiles(jnp.where(top_is_far, last, 0))

    def one_step(step, carry):
        for sim in range(2):
            def far_side():
                def odd():
                    top_rows(step, sim, FAR_ROWS, True)

                def even():
                    bottom_rows(step, sim, FAR_ROWS, True)

                by_side(odd, even)

            def near_side():
                if sim == 0:
                    @pl.when(step == 0)
                    def _():
                        lax.fori_loop(0, last, place_rest, 0)
                for layer in range(1, last):
                    electric_rows(step, sim, layer, 0, width_y)

                def odd():
                    bottom_rows(step, sim, width_y, False)
                    share_out(step, sim, 0, pl.ds(0, last), 0, width_y)

                def even():
                    top_rows(step, sim, width_y, False)
                    share_out(step, sim, 0, pl.ds(1, last), 0, width_y)

                by_side(odd, even)

            def one_side(turn, carry):
                far_turn = turn == jnp.where(step == 0, 0, 1)
                pl.when(far_turn)(far_side)
                pl.when(jnp.logical_not(far_turn))(near_side)
                return carry

            lax.fori_loop(0, 2, one_side, 0)

            @pl.when(step < steps - 1)
            def _():
                magnetic_inside(sim)
        return carry

    lax.fori_loop(0, steps, one_step, 0)

    def faces_gone(up_rows):
        @pl.when(has_above)
        def _():
            for sim in range(2):
                for lo in pieces(up_rows):
                    up_copy(0, sim, lo, up_rows).wait_send()

    by_side(lambda: faces_gone(FAR_ROWS), lambda: faces_gone(width_y))
    lax.fori_loop(1, slabs, tiles_gone, 0)

    def add_shares(parts):
        for k in range(1, port_devices):
            for group, layers in enumerate(parts):
                share_copy(k, group, layers).wait_recv()
        total = summed[:, share_span(port)]
        for k in range(1, port_devices):
            total = total + shares[k]
        result[...] = total * (1.0 / math.sqrt(ports_ref.shape[1] * steps))
        for k in range(1, port_devices):
            for group, layers in enumerate(parts):
                share_copy(k, group, layers).wait_send()

    by_side(
        lambda: add_shares((pl.ds(0, last), pl.ds(last, 1))),
        lambda: add_shares((pl.ds(1, last), pl.ds(0, 1))))


def store_kernel(elec, magn, total, out_fields, out_sens, sem):
    rows = out_fields.shape[4]
    copies = [pltpu.make_async_copy(total, out_sens, sem.at[0])]
    for sim in range(2):
        for comp in range(3):
            copies.append(pltpu.make_async_copy(
                elec.at[sim, comp, :, pl.ds(0, rows)], out_fields.at[sim, 0, comp], sem.at[len(copies)]))
            copies.append(pltpu.make_async_copy(
                magn.at[sim, comp, :, pl.ds(PAD, rows)], out_fields.at[sim, 0, 3 + comp], sem.at[len(copies)]))
    for copy in copies:
        copy.start()
    for copy in copies:
        copy.wait()


def solution(mesh):
    slabs, port_devices = mesh.shape["space"], mesh.shape["port"]

    def local(fields, inv_eps, tensor_tiles, tile_index, ports, waves):
        assert fields.shape[1] == 1
        width_x, width_y, width_z = fields.shape[3:]
        steps = waves.shape[2]
        slots = tile_index.shape[2]
        owner_rows = tensor_tiles.shape[2]
        share_rows = width_y // port_devices
        far_pieces = width_y // FAR_ROWS
        f32 = jnp.float32
        dma = pltpu.SemaphoreType.DMA
        held = pl.BlockSpec(memory_space=pltpu.HBM)
        onchip = pl.BlockSpec(memory_space=pltpu.VMEM)
        anywhere = pl.BlockSpec(memory_space=pl.ANY)
        state = pl.pallas_call(
            functools.partial(kernel, slabs, port_devices),
            out_shape=(
                pltpu.VMEM((2, 3, width_x, width_y + PAD, width_z), f32),
                pltpu.VMEM((2, 3, width_x, width_y + PAD, width_z), f32),
                pltpu.VMEM((width_x, share_rows, width_z), f32),
            ),
            in_specs=[held] * 6,
            out_specs=(onchip, onchip, onchip),
            scratch_shapes=[
                pltpu.SMEM(ports.shape, jnp.int32),
                pltpu.SMEM(waves.shape, f32),
                pltpu.VMEM((steps, 2, 2, width_y, width_z), f32),
                pltpu.VMEM((steps, 2, 2, width_y, width_z), f32),
                pltpu.VMEM((2, 2, width_y, width_z), f32),
                pltpu.VMEM((6, 3 * slabs * slots, width_z), jnp.bfloat16),
                pltpu.VMEM((6, width_x, width_y, width_z), f32),
                pltpu.VMEM((3, width_x, width_y, width_z), f32),
                pltpu.VMEM((slabs * owner_rows, width_z), f32),
                pltpu.VMEM((slots, slabs), jnp.int32),
                pltpu.VMEM((width_x * width_y, 3 * slabs * slots), jnp.bfloat16),
                pltpu.VMEM((width_x * width_y, width_z), f32),
                pltpu.VMEM((width_x, width_y, width_z), f32),
                pltpu.VMEM((port_devices, width_x, share_rows, width_z), f32),
                dma((7,)),
                dma((slabs,)),
                dma((slabs,)),
                dma((2, far_pieces)),
                dma((steps, 2, far_pieces)),
                dma((2, far_pieces)),
                dma((steps, 2, far_pieces)),
                dma((port_devices, 2)),
                dma((port_devices, 2)),
                pltpu.SemaphoreType.REGULAR((GROUPS,)),
                pltpu.SemaphoreType.REGULAR,
            ],
            compiler_params=pltpu.CompilerParams(
                collective_id=0, has_side_effects=True, vmem_limit_bytes=40 * 1024 * 1024),
            name="window",
        )(*[pltpu.with_memory_space_constraint(x, pltpu.HBM) for x in (ports, waves, fields, inv_eps, tensor_tiles, tile_index.transpose(0, 2, 1))])
        return pl.pallas_call(
            store_kernel,
            out_shape=(
                jax.ShapeDtypeStruct(fields.shape, f32),
                jax.ShapeDtypeStruct((width_x, share_rows, width_z), f32),
            ),
            in_specs=[anywhere] * 3,
            out_specs=(anywhere, anywhere),
            scratch_shapes=[dma((13,))],
            compiler_params=pltpu.CompilerParams(vmem_limit_bytes=4 * 1024 * 1024),
            name="store",
        )(*[pltpu.with_memory_space_constraint(x, pltpu.VMEM) for x in state])

    in_specs = (
        P(None, "port", None, "space", None, None),
        P(None, "space", None, None),
        P("space", None, None, None),
        P("space", None, None),
        P(),
        P(None, "port", None),
    )
    out_specs = (P(None, "port", None, "space", None, None), P("space", "port", None))
    return jax.shard_map(local, mesh=mesh, in_specs=in_specs, out_specs=out_specs, check_vma=False)
```

```python
import functools
import math

import jax
import jax.numpy as jnp
from jax import lax
from jax.experimental import pallas as pl
from jax.experimental.pallas import tpu as pltpu
from jax.sharding import PartitionSpec as P

MESH = pl.DeviceIdType.MESH
magnetic_coef = 0.5
PAD = 8
ROWS = 8
FAR_ROWS = 16
GROUPS = 4


def kernel(
    slabs, port_devices, ports_in, waves_in, fields, inv_eps, tiles, tile_index,
    elec, magn, result,
    ports_ref, waves_ref, face_up, face_down, partial, pieces_ref, tensor, bulk, arrived, index, onehot, live, summed,
    shares, load_sem, tile_send, tile_recv, up_send, up_recv, down_send, down_recv,
    share_send, share_recv, ready, port_ready,
):
    me = lax.axis_index("space")
    port = lax.axis_index("port")
    width_x, width_y, width_z = inv_eps.shape[1:]
    steps = waves_ref.shape[2]
    last = width_x - 1
    owner_rows = tiles.shape[2]
    slots = owner_rows // 6
    share_rows = width_y // port_devices
    has_below = me > 0
    has_above = me < slabs - 1
    above = jnp.minimum(me + 1, slabs - 1)
    below = jnp.maximum(me - 1, 0)

    def owner_span(owner):
        return pl.ds(pl.multiple_of(owner * owner_rows, 8), owner_rows)

    barrier = pltpu.get_barrier_semaphore()

    size = slabs // GROUPS
    group = me // size

    def signal(semaphore, slab, along):
        pl.semaphore_signal(semaphore, inc=1, device_id=(slab, along), device_id_type=MESH)

    def await_all(semaphore, count):
        @pl.when(count > 0)
        def _():
            pl.semaphore_wait(semaphore, count)

    def each(low, high, act):
        def body(slab, carry):
            act(slab)
            return carry
        lax.fori_loop(low, high, body, 0)

    each(me + 1, slabs, lambda slab: signal(barrier, slab, port))
    each(port + 1, port_devices, lambda along: signal(barrier, me, along))

    loads = [
        pltpu.make_async_copy(fields.at[:, 0, pl.ds(0, 3)], elec.at[:, :, :, pl.ds(0, width_y)], load_sem.at[0]),
        pltpu.make_async_copy(fields.at[:, 0, pl.ds(3, 3)], magn.at[:, :, :, pl.ds(PAD, width_y)], load_sem.at[1]),
        pltpu.make_async_copy(inv_eps, bulk, load_sem.at[2]),
        pltpu.make_async_copy(tile_index.at[0], index, load_sem.at[3]),
        pltpu.make_async_copy(tiles.at[0, me], arrived.at[owner_span(me)], load_sem.at[4]),
        pltpu.make_async_copy(ports_in, ports_ref, load_sem.at[5]),
        pltpu.make_async_copy(waves_in, waves_ref, load_sem.at[6]),
    ]
    for load in (loads[3], loads[5], loads[6], loads[0], loads[1], loads[2], loads[4]):
        load.start()

    def up_copy(step, sim, lo, rows):
        span, k = pl.ds(lo, rows), lo // rows
        return pltpu.make_async_remote_copy(
            partial.at[sim, :, span], face_down.at[step, sim, :, span],
            up_send.at[sim, k], up_recv.at[step, sim, k], device_id=(above, port), device_id_type=MESH)

    def down_copy(step, sim, lo, rows):
        span, k = pl.ds(lo, rows), lo // rows
        return pltpu.make_async_remote_copy(
            elec.at[sim, pl.ds(1, 2), 0, span], face_up.at[step, sim, :, span],
            down_send.at[sim, k], down_recv.at[step, sim, k], device_id=(below, port), device_id_type=MESH)

    top_is_far = lax.rem(me, 2) == 1

    def by_side(odd, even):
        pl.when(top_is_far)(odd)
        pl.when(jnp.logical_not(top_is_far))(even)

    def pieces(rows):
        return range(0, width_y, rows)

    def tile_copy(k):
        target = lax.rem(me + k, slabs)
        return pltpu.make_async_remote_copy(
            tiles.at[0, target], arrived.at[owner_span(me)],
            tile_send.at[k], tile_recv.at[k], device_id=(target, port), device_id_type=MESH)

    def send_tile(slab):
        tile_copy(lax.rem(slab - me + slabs, slabs)).start()

    await_all(barrier, me + port)
    each(0, me, lambda slab: signal(ready.at[group - slab // size], slab, port))
    each(0, port, lambda along: signal(port_ready, me, along))
    each(0, me, send_tile)

    for offset in range(1):
        ahead = group + offset

        @pl.when(ahead < GROUPS)
        def _():
            low = jnp.maximum(ahead * size, me + 1)
            high = (ahead + 1) * size
            await_all(ready.at[offset], high - low)
            each(low, high, send_tile)

    zero_rows = jnp.zeros((PAD, width_z), jnp.float32)
    for sim in range(2):
        for comp in range(3):
            for layer in range(width_x):
                elec[sim, comp, layer, pl.ds(width_y, PAD)] = zero_rows
                magn[sim, comp, layer, pl.ds(0, PAD)] = zero_rows
    zero_plane = jnp.zeros((width_y, width_z), jnp.float32)

    @pl.when(me == 0)
    def _():
        def clear(step, carry):
            for sim in range(2):
                for comp in range(2):
                    face_down[step, sim, comp] = zero_plane
            return carry
        lax.fori_loop(0, steps, clear, 0)

    @pl.when(me == slabs - 1)
    def _():
        def clear(step, carry):
            for sim in range(2):
                for comp in range(2):
                    face_up[step, sim, comp] = zero_plane
            return carry
        lax.fori_loop(0, steps, clear, 0)

    for layer in range(width_x):
        summed[layer] = zero_plane

    columns = width_x * width_y
    loads[3].wait()
    spots_down = lax.broadcasted_iota(jnp.int32, (columns, slabs), 0)
    for k in range(slots):
        marks = jnp.where(index[k : k + 1, :] == spots_down, 1.0, 0.0).astype(jnp.bfloat16)
        for part in range(3):
            onehot[:, (part * slots + k) * slabs : (part * slots + k + 1) * slabs] = marks
    live[...] = jnp.dot(
        onehot[...], jnp.ones((3 * slabs * slots, width_z), jnp.bfloat16), preferred_element_type=jnp.float32)

    lane = lax.broadcasted_iota(jnp.int32, (ROWS, width_z), 1)
    row = lax.broadcasted_iota(jnp.int32, (ROWS, width_z), 0)
    cell_ids = row * width_z + lane
    not_last = lane < width_z - 1
    not_first = lane > 0
    plane = width_y * width_z
    loads[5].wait()
    loads[6].wait()
    source_cell = [ports_ref[sim, port] - me * (width_x * plane) for sim in range(2)]

    def next_z(values):
        return jnp.where(not_last, pltpu.roll(values, width_z - 1, 1), 0.0)

    def prev_z(values):
        return jnp.where(not_first, pltpu.roll(values, 1, 1), 0.0)

    def magnetic_rows(sim, layer, lo, rows):
        for y in range(lo, lo + rows, ROWS):
            at, nxt, hat = pl.ds(y, ROWS), pl.ds(y + 1, ROWS), pl.ds(PAD + y, ROWS)
            ey = elec[sim, 1, layer, at]
            ez = elec[sim, 2, layer, at]
            magn[sim, 0, layer, hat] = magn[sim, 0, layer, hat] - magnetic_coef * (
                elec[sim, 2, layer, nxt] - ez - (next_z(ey) - ey))
            if layer < last:
                ex = elec[sim, 0, layer, at]
                magn[sim, 1, layer, hat] = magn[sim, 1, layer, hat] - magnetic_coef * (
                    next_z(ex) - ex - (elec[sim, 2, layer + 1, at] - ez))
                magn[sim, 2, layer, hat] = magn[sim, 2, layer, hat] - magnetic_coef * (
                    elec[sim, 1, layer + 1, at] - ey - (elec[sim, 0, layer, nxt] - ex))

    def magnetic_last(step, sim, lo, rows):
        for y in range(lo, lo + rows, ROWS):
            at, hat = pl.ds(y, ROWS), pl.ds(PAD + y, ROWS)
            magn[sim, 1, last, hat] = partial[sim, 0, at] + magnetic_coef * face_up[step, sim, 1, at]
            magn[sim, 2, last, hat] = partial[sim, 1, at] - magnetic_coef * face_up[step, sim, 0, at]

    def partial_rows(sim, lo, rows):
        for y in range(lo, lo + rows, ROWS):
            at, nxt, hat = pl.ds(y, ROWS), pl.ds(y + 1, ROWS), pl.ds(PAD + y, ROWS)
            ex = elec[sim, 0, last, at]
            partial[sim, 0, at] = magn[sim, 1, last, hat] - magnetic_coef * (
                next_z(ex) - ex + elec[sim, 2, last, at])
            partial[sim, 1, at] = magn[sim, 2, last, hat] + magnetic_coef * (
                elec[sim, 1, last, at] + (elec[sim, 0, last, nxt] - ex))

    halo_coef = jnp.where(has_below, magnetic_coef, 0.0).astype(jnp.float32)

    def electric_rows(step, sim, layer, lo, rows):
        pulse = waves_ref[sim, 0, step]
        for y in range(lo, lo + rows, ROWS):
            at, hat, prv = pl.ds(y, ROWS), pl.ds(PAD + y, ROWS), pl.ds(PAD + y - 1, ROWS)
            hx = magn[sim, 0, layer, hat]
            hy = magn[sim, 1, layer, hat]
            hz = magn[sim, 2, layer, hat]
            ex = elec[sim, 0, layer, at]
            ey = elec[sim, 1, layer, at]
            ez = elec[sim, 2, layer, at]
            if layer > 0:
                hy_down, hz_down = magn[sim, 1, layer - 1, hat], magn[sim, 2, layer - 1, hat]
            else:
                hy_down = face_down[step, sim, 0, at] + halo_coef * ez
                hz_down = face_down[step, sim, 1, at] - halo_coef * ey
            cx = hz - magn[sim, 2, layer, prv] - (hy - prev_z(hy))
            cy = hx - prev_z(hx) - (hz - hz_down)
            cz = hy - hy_down - (hx - magn[sim, 0, layer, prv])
            xy, xz, yz = tensor[3, layer, at], tensor[4, layer, at], tensor[5, layer, at]
            ex = ex + (tensor[0, layer, at] * cx + xy * cy + xz * cz)
            ey = ey + (xy * cx + tensor[1, layer, at] * cy + yz * cz)
            ez = ez + (xz * cx + yz * cy + tensor[2, layer, at] * cz)
            here = source_cell[sim] - (layer * plane + y * width_z)
            ez = ez + jnp.where(cell_ids == here, pulse, 0.0)
            elec[sim, 0, layer, at] = ex
            elec[sim, 1, layer, at] = ey
            elec[sim, 2, layer, at] = ez
            if sim == 1:
                summed[layer, at] = summed[layer, at] + (
                    elec[0, 0, layer, at] * ex + elec[0, 1, layer, at] * ey + elec[0, 2, layer, at] * ez)

    loads[0].wait()
    loads[1].wait()
    for sim in range(2):
        partial_rows(sim, 0, width_y)

    for offset in range(1, GROUPS):
        ahead = group + offset

        @pl.when(ahead < GROUPS)
        def _():
            low = jnp.maximum(ahead * size, me + 1)
            high = (ahead + 1) * size
            await_all(ready.at[offset], high - low)
            each(low, high, send_tile)

    def first_faces(up_rows, down_rows):
        @pl.when(has_above)
        def _():
            for sim in range(2):
                for lo in pieces(up_rows):
                    up_copy(0, sim, lo, up_rows).start()

        @pl.when(has_below)
        def _():
            for sim in range(2):
                for lo in pieces(down_rows):
                    down_copy(0, sim, lo, down_rows).start()

    by_side(lambda: first_faces(FAR_ROWS, width_y), lambda: first_faces(width_y, FAR_ROWS))

    def magnetic_inside(sim):
        for layer in range(width_x):
            magnetic_rows(sim, layer, 0, width_y)

    for sim in range(2):
        magnetic_inside(sim)
    loads[2].wait()
    loads[4].wait()

    def take_tiles(k, carry):
        tile_copy(k).wait_recv()
        return carry

    def tiles_gone(k, carry):
        tile_copy(k).wait_send()
        return carry

    def split_tiles():
        for entry in range(6):
            block = jnp.concatenate(
                [arrived[pl.ds(6 * k + entry, slabs, stride=owner_rows), :] for k in range(slots)], 0)
            high = block.astype(jnp.bfloat16)
            rest = block - high.astype(jnp.float32)
            middle = rest.astype(jnp.bfloat16)
            low = (rest - middle.astype(jnp.float32)).astype(jnp.bfloat16)
            for part, values in enumerate((high, middle, low)):
                pieces_ref[entry, part * slots * slabs : (part + 1) * slots * slabs] = values

    def place_tiles(layer):
        rows = pl.ds(pl.multiple_of(layer * width_y, 16), width_y)
        spots = onehot[rows, :]
        taken = live[rows, :] > 0.5
        for entry in range(6):
            placed = jnp.dot(spots, pieces_ref[entry], preferred_element_type=jnp.float32)
            tensor[entry, layer] = jnp.where(taken, placed, bulk[entry, layer] if entry < 3 else 0.0)

    def place_rest(k, carry):
        place_tiles(k + jnp.where(top_is_far, 0, 1))
        return carry

    def share_span(device):
        return pl.ds(pl.multiple_of(device * share_rows, 8), share_rows)

    def share_copy(k, group, layers):
        target = lax.rem(port + k, port_devices)
        return pltpu.make_async_remote_copy(
            summed.at[layers, share_span(target)], shares.at[k, layers],
            share_send.at[k, group], share_recv.at[k, group], device_id=(me, target), device_id_type=MESH)

    def share_out(step, sim, group, layers, lo, rows):
        if sim == 1:
            for k in range(1, port_devices):
                end = (lax.rem(port + k, port_devices) + 1) * share_rows

                @pl.when((step == steps - 1) & (end > lo) & (end <= lo + rows))
                def _():
                    share_copy(k, group, layers).start()

    def top_rows(step, sim, rows, far):
        def send(lo):
            @pl.when(step < steps - 1)
            def _():
                @pl.when(has_above)
                def _():
                    up_copy(step, sim, lo, rows).wait_send()
                partial_rows(sim, lo, rows)

                @pl.when(has_above)
                def _():
                    up_copy(step + 1, sim, lo, rows).start()

        for lo in pieces(rows):
            @pl.when(has_above)
            def _():
                down_copy(step, sim, lo, rows).wait_recv()
            magnetic_last(step, sim, lo, rows)
            electric_rows(step, sim, last, lo, rows)
            if far:
                share_out(step, sim, 1, pl.ds(last, 1), lo, rows)
            if lo > 0:
                send(lo - rows)
        send(width_y - rows)

    def bottom_rows(step, sim, rows, far):
        for lo in pieces(rows):
            @pl.when(has_below)
            def _():
                up_copy(step, sim, lo, rows).wait_recv()
                down_copy(step, sim, lo, rows).wait_send()
            electric_rows(step, sim, 0, lo, rows)
            if far:
                share_out(step, sim, 1, pl.ds(0, 1), lo, rows)

            @pl.when(jnp.logical_and(has_below, step < steps - 1))
            def _():
                down_copy(step + 1, sim, lo, rows).start()

    lax.fori_loop(1, slabs, take_tiles, 0)
    await_all(port_ready, port_devices - 1 - port)
    split_tiles()
    place_tiles(jnp.where(top_is_far, last, 0))

    def one_step(step, carry):
        for sim in range(2):
            def far_side():
                def odd():
                    top_rows(step, sim, FAR_ROWS, True)

                def even():
                    bottom_rows(step, sim, FAR_ROWS, True)

                by_side(odd, even)

            def near_side():
                if sim == 0:
                    @pl.when(step == 0)
                    def _():
                        lax.fori_loop(0, last, place_rest, 0)
                for layer in range(1, last):
                    electric_rows(step, sim, layer, 0, width_y)

                def odd():
                    bottom_rows(step, sim, width_y, False)
                    share_out(step, sim, 0, pl.ds(0, last), 0, width_y)

                def even():
                    top_rows(step, sim, width_y, False)
                    share_out(step, sim, 0, pl.ds(1, last), 0, width_y)

                by_side(odd, even)

            def one_side(turn, carry):
                far_turn = turn == jnp.where(step == 0, 0, 1)
                pl.when(far_turn)(far_side)
                pl.when(jnp.logical_not(far_turn))(near_side)
                return carry

            lax.fori_loop(0, 2, one_side, 0)

            @pl.when(step < steps - 1)
            def _():
                magnetic_inside(sim)
        return carry

    lax.fori_loop(0, steps, one_step, 0)

    def faces_gone(up_rows):
        @pl.when(has_above)
        def _():
            for sim in range(2):
                for lo in pieces(up_rows):
                    up_copy(0, sim, lo, up_rows).wait_send()

    by_side(lambda: faces_gone(FAR_ROWS), lambda: faces_gone(width_y))
    lax.fori_loop(1, slabs, tiles_gone, 0)

    def add_shares(parts):
        for k in range(1, port_devices):
            for group, layers in enumerate(parts):
                share_copy(k, group, layers).wait_recv()
        total = summed[:, share_span(port)]
        for k in range(1, port_devices):
            total = total + shares[k]
        result[...] = total * (1.0 / math.sqrt(ports_ref.shape[1] * steps))
        for k in range(1, port_devices):
            for group, layers in enumerate(parts):
                share_copy(k, group, layers).wait_send()

    by_side(
        lambda: add_shares((pl.ds(0, last), pl.ds(last, 1))),
        lambda: add_shares((pl.ds(1, last), pl.ds(0, 1))))


def store_kernel(elec, magn, total, out_fields, out_sens, sem):
    rows = out_fields.shape[4]
    copies = [pltpu.make_async_copy(total, out_sens, sem.at[0])]
    for sim in range(2):
        for comp in range(3):
            copies.append(pltpu.make_async_copy(
                elec.at[sim, comp, :, pl.ds(0, rows)], out_fields.at[sim, 0, comp], sem.at[len(copies)]))
            copies.append(pltpu.make_async_copy(
                magn.at[sim, comp, :, pl.ds(PAD, rows)], out_fields.at[sim, 0, 3 + comp], sem.at[len(copies)]))
    for copy in copies:
        copy.start()
    for copy in copies:
        copy.wait()


def solution(mesh):
    slabs, port_devices = mesh.shape["space"], mesh.shape["port"]

    def local(fields, inv_eps, tensor_tiles, tile_index, ports, waves):
        assert fields.shape[1] == 1
        width_x, width_y, width_z = fields.shape[3:]
        steps = waves.shape[2]
        slots = tile_index.shape[2]
        owner_rows = tensor_tiles.shape[2]
        share_rows = width_y // port_devices
        far_pieces = width_y // FAR_ROWS
        f32 = jnp.float32
        dma = pltpu.SemaphoreType.DMA
        held = pl.BlockSpec(memory_space=pltpu.HBM)
        onchip = pl.BlockSpec(memory_space=pltpu.VMEM)
        anywhere = pl.BlockSpec(memory_space=pl.ANY)
        state = pl.pallas_call(
            functools.partial(kernel, slabs, port_devices),
            out_shape=(
                pltpu.VMEM((2, 3, width_x, width_y + PAD, width_z), f32),
                pltpu.VMEM((2, 3, width_x, width_y + PAD, width_z), f32),
                pltpu.VMEM((width_x, share_rows, width_z), f32),
            ),
            in_specs=[held] * 6,
            out_specs=(onchip, onchip, onchip),
            scratch_shapes=[
                pltpu.SMEM(ports.shape, jnp.int32),
                pltpu.SMEM(waves.shape, f32),
                pltpu.VMEM((steps, 2, 2, width_y, width_z), f32),
                pltpu.VMEM((steps, 2, 2, width_y, width_z), f32),
                pltpu.VMEM((2, 2, width_y, width_z), f32),
                pltpu.VMEM((6, 3 * slabs * slots, width_z), jnp.bfloat16),
                pltpu.VMEM((6, width_x, width_y, width_z), f32),
                pltpu.VMEM((3, width_x, width_y, width_z), f32),
                pltpu.VMEM((slabs * owner_rows, width_z), f32),
                pltpu.VMEM((slots, slabs), jnp.int32),
                pltpu.VMEM((width_x * width_y, 3 * slabs * slots), jnp.bfloat16),
                pltpu.VMEM((width_x * width_y, width_z), f32),
                pltpu.VMEM((width_x, width_y, width_z), f32),
                pltpu.VMEM((port_devices, width_x, share_rows, width_z), f32),
                dma((7,)),
                dma((slabs,)),
                dma((slabs,)),
                dma((2, far_pieces)),
                dma((steps, 2, far_pieces)),
                dma((2, far_pieces)),
                dma((steps, 2, far_pieces)),
                dma((port_devices, 2)),
                dma((port_devices, 2)),
                pltpu.SemaphoreType.REGULAR((GROUPS,)),
                pltpu.SemaphoreType.REGULAR,
            ],
            compiler_params=pltpu.CompilerParams(
                collective_id=0, has_side_effects=True, vmem_limit_bytes=40 * 1024 * 1024),
            name="window",
        )(*[pltpu.with_memory_space_constraint(x, pltpu.HBM) for x in (ports, waves, fields, inv_eps, tensor_tiles, tile_index.transpose(0, 2, 1))])
        return pl.pallas_call(
            store_kernel,
            out_shape=(
                jax.ShapeDtypeStruct(fields.shape, f32),
                jax.ShapeDtypeStruct((width_x, share_rows, width_z), f32),
            ),
            in_specs=[anywhere] * 3,
            out_specs=(anywhere, anywhere),
            scratch_shapes=[dma((13,))],
            compiler_params=pltpu.CompilerParams(vmem_limit_bytes=4 * 1024 * 1024),
            name="store",
        )(*[pltpu.with_memory_space_constraint(x, pltpu.VMEM) for x in state])

    in_specs = (
        P(None, "port", None, "space", None, None),
        P(None, "space", None, None),
        P("space", None, None, None),
        P("space", None, None),
        P(),
        P(None, "port", None),
    )
    out_specs = (P(None, "port", None, "space", None, None), P("space", "port", None))
    return jax.shard_map(local, mesh=mesh, in_specs=in_specs, out_specs=out_specs, check_vma=False)
```

```python
import functools
import math

import jax
import jax.numpy as jnp
from jax import lax
from jax.experimental import pallas as pl
from jax.experimental.pallas import tpu as pltpu
from jax.sharding import PartitionSpec as P

MESH = pl.DeviceIdType.MESH
magnetic_coef = 0.5
PAD = 8
ROWS = 8
FAR_ROWS = 16
GROUPS = 4


def kernel(
    slabs, port_devices, ports_in, waves_in, fields, inv_eps, tiles, tile_index,
    elec, magn, result,
    ports_ref, waves_ref, face_up, face_down, partial, pieces_ref, tensor, bulk, arrived, index, onehot, live, summed,
    shares, load_sem, tile_send, tile_recv, up_send, up_recv, down_send, down_recv,
    share_send, share_recv, ready, port_ready,
):
    me = lax.axis_index("space")
    port = lax.axis_index("port")
    width_x, width_y, width_z = inv_eps.shape[1:]
    steps = waves_ref.shape[2]
    last = width_x - 1
    owner_rows = tiles.shape[2]
    slots = owner_rows // 6
    share_rows = width_y // port_devices
    has_below = me > 0
    has_above = me < slabs - 1
    above = jnp.minimum(me + 1, slabs - 1)
    below = jnp.maximum(me - 1, 0)

    def owner_span(owner):
        return pl.ds(pl.multiple_of(owner * owner_rows, 8), owner_rows)

    barrier = pltpu.get_barrier_semaphore()

    size = slabs // GROUPS
    group = me // size

    def signal(semaphore, slab, along):
        pl.semaphore_signal(semaphore, inc=1, device_id=(slab, along), device_id_type=MESH)

    def await_all(semaphore, count):
        @pl.when(count > 0)
        def _():
            pl.semaphore_wait(semaphore, count)

    def each(low, high, act):
        def body(slab, carry):
            act(slab)
            return carry
        lax.fori_loop(low, high, body, 0)

    each(me + 1, slabs, lambda slab: signal(barrier, slab, port))
    each(port + 1, port_devices, lambda along: signal(barrier, me, along))

    loads = [
        pltpu.make_async_copy(fields.at[:, 0, pl.ds(0, 3)], elec.at[:, :, :, pl.ds(0, width_y)], load_sem.at[0]),
        pltpu.make_async_copy(fields.at[:, 0, pl.ds(3, 3)], magn.at[:, :, :, pl.ds(PAD, width_y)], load_sem.at[1]),
        pltpu.make_async_copy(inv_eps, bulk, load_sem.at[2]),
        pltpu.make_async_copy(tile_index.at[0], index, load_sem.at[3]),
        pltpu.make_async_copy(tiles.at[0, me], arrived.at[owner_span(me)], load_sem.at[4]),
        pltpu.make_async_copy(ports_in, ports_ref, load_sem.at[5]),
        pltpu.make_async_copy(waves_in, waves_ref, load_sem.at[6]),
    ]
    for load in (loads[3], loads[5], loads[6], loads[0], loads[1], loads[2], loads[4]):
        load.start()

    def up_copy(step, sim, lo, rows):
        span, k = pl.ds(lo, rows), lo // rows
        return pltpu.make_async_remote_copy(
            partial.at[sim, :, span], face_down.at[step, sim, :, span],
            up_send.at[sim, k], up_recv.at[step, sim, k], device_id=(above, port), device_id_type=MESH)

    def down_copy(step, sim, lo, rows):
        span, k = pl.ds(lo, rows), lo // rows
        return pltpu.make_async_remote_copy(
            elec.at[sim, pl.ds(1, 2), 0, span], face_up.at[step, sim, :, span],
            down_send.at[sim, k], down_recv.at[step, sim, k], device_id=(below, port), device_id_type=MESH)

    top_is_far = lax.rem(me, 2) == 1

    def by_side(odd, even):
        pl.when(top_is_far)(odd)
        pl.when(jnp.logical_not(top_is_far))(even)

    def pieces(rows):
        return range(0, width_y, rows)

    def tile_copy(k):
        target = lax.rem(me + k, slabs)
        return pltpu.make_async_remote_copy(
            tiles.at[0, target], arrived.at[owner_span(me)],
            tile_send.at[k], tile_recv.at[k], device_id=(target, port), device_id_type=MESH)

    def send_tile(slab):
        tile_copy(lax.rem(slab - me + slabs, slabs)).start()

    await_all(barrier, me + port)
    each(0, me, lambda slab: signal(ready.at[group - slab // size], slab, port))
    each(0, port, lambda along: signal(port_ready, me, along))
    each(0, me, send_tile)

    for offset in range(1):
        ahead = group + offset

        @pl.when(ahead < GROUPS)
        def _():
            low = jnp.maximum(ahead * size, me + 1)
            high = (ahead + 1) * size
            await_all(ready.at[offset], high - low)
            each(low, high, send_tile)

    zero_rows = jnp.zeros((PAD, width_z), jnp.float32)
    for sim in range(2):
        for comp in range(3):
            for layer in range(width_x):
                elec[sim, comp, layer, pl.ds(width_y, PAD)] = zero_rows
                magn[sim, comp, layer, pl.ds(0, PAD)] = zero_rows
    zero_plane = jnp.zeros((width_y, width_z), jnp.float32)

    @pl.when(me == 0)
    def _():
        def clear(step, carry):
            for sim in range(2):
                for comp in range(2):
                    face_down[step, sim, comp] = zero_plane
            return carry
        lax.fori_loop(0, steps, clear, 0)

    @pl.when(me == slabs - 1)
    def _():
        def clear(step, carry):
            for sim in range(2):
                for comp in range(2):
                    face_up[step, sim, comp] = zero_plane
            return carry
        lax.fori_loop(0, steps, clear, 0)

    for layer in range(width_x):
        summed[layer] = zero_plane

    columns = width_x * width_y
    loads[3].wait()
    spots_down = lax.broadcasted_iota(jnp.int32, (columns, slabs), 0)
    for k in range(slots):
        marks = jnp.where(index[k : k + 1, :] == spots_down, 1.0, 0.0).astype(jnp.bfloat16)
        for part in range(3):
            onehot[:, (part * slots + k) * slabs : (part * slots + k + 1) * slabs] = marks
    live[...] = jnp.dot(
        onehot[...], jnp.ones((3 * slabs * slots, width_z), jnp.bfloat16), preferred_element_type=jnp.float32)

    lane = lax.broadcasted_iota(jnp.int32, (ROWS, width_z), 1)
    row = lax.broadcasted_iota(jnp.int32, (ROWS, width_z), 0)
    cell_ids = row * width_z + lane
    not_last = lane < width_z - 1
    not_first = lane > 0
    plane = width_y * width_z
    loads[5].wait()
    loads[6].wait()
    source_cell = [ports_ref[sim, port] - me * (width_x * plane) for sim in range(2)]

    def next_z(values):
        return jnp.where(not_last, pltpu.roll(values, width_z - 1, 1), 0.0)

    def prev_z(values):
        return jnp.where(not_first, pltpu.roll(values, 1, 1), 0.0)

    def magnetic_rows(sim, layer, lo, rows):
        for y in range(lo, lo + rows, ROWS):
            at, nxt, hat = pl.ds(y, ROWS), pl.ds(y + 1, ROWS), pl.ds(PAD + y, ROWS)
            ey = elec[sim, 1, layer, at]
            ez = elec[sim, 2, layer, at]
            magn[sim, 0, layer, hat] = magn[sim, 0, layer, hat] - magnetic_coef * (
                elec[sim, 2, layer, nxt] - ez - (next_z(ey) - ey))
            if layer < last:
                ex = elec[sim, 0, layer, at]
                magn[sim, 1, layer, hat] = magn[sim, 1, layer, hat] - magnetic_coef * (
                    next_z(ex) - ex - (elec[sim, 2, layer + 1, at] - ez))
                magn[sim, 2, layer, hat] = magn[sim, 2, layer, hat] - magnetic_coef * (
                    elec[sim, 1, layer + 1, at] - ey - (elec[sim, 0, layer, nxt] - ex))

    def magnetic_last(step, sim, lo, rows):
        for y in range(lo, lo + rows, ROWS):
            at, hat = pl.ds(y, ROWS), pl.ds(PAD + y, ROWS)
            magn[sim, 1, last, hat] = partial[sim, 0, at] + magnetic_coef * face_up[step, sim, 1, at]
            magn[sim, 2, last, hat] = partial[sim, 1, at] - magnetic_coef * face_up[step, sim, 0, at]

    def partial_rows(sim, lo, rows):
        for y in range(lo, lo + rows, ROWS):
            at, nxt, hat = pl.ds(y, ROWS), pl.ds(y + 1, ROWS), pl.ds(PAD + y, ROWS)
            ex = elec[sim, 0, last, at]
            partial[sim, 0, at] = magn[sim, 1, last, hat] - magnetic_coef * (
                next_z(ex) - ex + elec[sim, 2, last, at])
            partial[sim, 1, at] = magn[sim, 2, last, hat] + magnetic_coef * (
                elec[sim, 1, last, at] + (elec[sim, 0, last, nxt] - ex))

    def electric_first(step, sim, lo, rows):
        for y in range(lo, lo + rows, ROWS):
            at = pl.ds(y, ROWS)
            hy, hz = face_down[step, sim, 0, at], face_down[step, sim, 1, at]
            xy, xz, yz = tensor[3, 0, at], tensor[4, 0, at], tensor[5, 0, at]
            ex = elec[sim, 0, 0, at] + (xy * hz - xz * hy)
            ey = elec[sim, 1, 0, at] + (tensor[1, 0, at] * hz - yz * hy)
            ez = elec[sim, 2, 0, at] + (yz * hz - tensor[2, 0, at] * hy)
            elec[sim, 0, 0, at] = ex
            elec[sim, 1, 0, at] = ey
            elec[sim, 2, 0, at] = ez
            if sim == 1:
                summed[0, at] = summed[0, at] + (
                    elec[0, 0, 0, at] * ex + elec[0, 1, 0, at] * ey + elec[0, 2, 0, at] * ez)

    halo_coef = jnp.where(has_below, magnetic_coef, 0.0).astype(jnp.float32)

    def electric_rows(step, sim, layer, lo, rows, ahead=False):
        pulse = waves_ref[sim, 0, step]
        for y in range(lo, lo + rows, ROWS):
            at, hat, prv = pl.ds(y, ROWS), pl.ds(PAD + y, ROWS), pl.ds(PAD + y - 1, ROWS)
            hx = magn[sim, 0, layer, hat]
            hy = magn[sim, 1, layer, hat]
            hz = magn[sim, 2, layer, hat]
            ex = elec[sim, 0, layer, at]
            ey = elec[sim, 1, layer, at]
            ez = elec[sim, 2, layer, at]
            if layer > 0:
                hy_down, hz_down = magn[sim, 1, layer - 1, hat], magn[sim, 2, layer - 1, hat]
            elif ahead:
                hy_down, hz_down = halo_coef * ez, -halo_coef * ey
            else:
                hy_down = face_down[step, sim, 0, at] + halo_coef * ez
                hz_down = face_down[step, sim, 1, at] - halo_coef * ey
            cx = hz - magn[sim, 2, layer, prv] - (hy - prev_z(hy))
            cy = hx - prev_z(hx) - (hz - hz_down)
            cz = hy - hy_down - (hx - magn[sim, 0, layer, prv])
            xy, xz, yz = tensor[3, layer, at], tensor[4, layer, at], tensor[5, layer, at]
            ex = ex + (tensor[0, layer, at] * cx + xy * cy + xz * cz)
            ey = ey + (xy * cx + tensor[1, layer, at] * cy + yz * cz)
            ez = ez + (xz * cx + yz * cy + tensor[2, layer, at] * cz)
            here = source_cell[sim] - (layer * plane + y * width_z)
            ez = ez + jnp.where(cell_ids == here, pulse, 0.0)
            elec[sim, 0, layer, at] = ex
            elec[sim, 1, layer, at] = ey
            elec[sim, 2, layer, at] = ez
            if sim == 1 and not ahead:
                summed[layer, at] = summed[layer, at] + (
                    elec[0, 0, layer, at] * ex + elec[0, 1, layer, at] * ey + elec[0, 2, layer, at] * ez)

    loads[0].wait()
    loads[1].wait()
    for sim in range(2):
        partial_rows(sim, 0, width_y)

    for offset in range(1, GROUPS):
        ahead = group + offset

        @pl.when(ahead < GROUPS)
        def _():
            low = jnp.maximum(ahead * size, me + 1)
            high = (ahead + 1) * size
            await_all(ready.at[offset], high - low)
            each(low, high, send_tile)

    def first_faces(up_rows, down_rows):
        @pl.when(has_above)
        def _():
            for sim in range(2):
                for lo in pieces(up_rows):
                    up_copy(0, sim, lo, up_rows).start()

        @pl.when(has_below)
        def _():
            for sim in range(2):
                for lo in pieces(down_rows):
                    down_copy(0, sim, lo, down_rows).start()

    by_side(lambda: first_faces(FAR_ROWS, width_y), lambda: first_faces(width_y, FAR_ROWS))

    def magnetic_inside(sim):
        for layer in range(width_x):
            magnetic_rows(sim, layer, 0, width_y)

    for sim in range(2):
        magnetic_inside(sim)
    loads[2].wait()
    loads[4].wait()

    def take_tiles(k, carry):
        tile_copy(k).wait_recv()
        return carry

    def tiles_gone(k, carry):
        tile_copy(k).wait_send()
        return carry

    def split_tiles():
        for entry in range(6):
            block = jnp.concatenate(
                [arrived[pl.ds(6 * k + entry, slabs, stride=owner_rows), :] for k in range(slots)], 0)
            high = block.astype(jnp.bfloat16)
            rest = block - high.astype(jnp.float32)
            middle = rest.astype(jnp.bfloat16)
            low = (rest - middle.astype(jnp.float32)).astype(jnp.bfloat16)
            for part, values in enumerate((high, middle, low)):
                pieces_ref[entry, part * slots * slabs : (part + 1) * slots * slabs] = values

    def place_tiles(layer):
        rows = pl.ds(pl.multiple_of(layer * width_y, 16), width_y)
        spots = onehot[rows, :]
        taken = live[rows, :] > 0.5
        for entry in range(6):
            placed = jnp.dot(spots, pieces_ref[entry], preferred_element_type=jnp.float32)
            tensor[entry, layer] = jnp.where(taken, placed, bulk[entry, layer] if entry < 3 else 0.0)

    def place_rest(k, carry):
        place_tiles(k + jnp.where(top_is_far, 0, 1))
        return carry

    def share_span(device):
        return pl.ds(pl.multiple_of(device * share_rows, 8), share_rows)

    def share_copy(k, group, layers):
        target = lax.rem(port + k, port_devices)
        return pltpu.make_async_remote_copy(
            summed.at[layers, share_span(target)], shares.at[k, layers],
            share_send.at[k, group], share_recv.at[k, group], device_id=(me, target), device_id_type=MESH)

    def share_out(step, sim, group, layers, lo, rows):
        if sim == 1:
            for k in range(1, port_devices):
                end = (lax.rem(port + k, port_devices) + 1) * share_rows

                @pl.when((step == steps - 1) & (end > lo) & (end <= lo + rows))
                def _():
                    share_copy(k, group, layers).start()

    def top_rows(step, sim, rows, far):
        def send(lo):
            @pl.when(step < steps - 1)
            def _():
                @pl.when(has_above)
                def _():
                    up_copy(step, sim, lo, rows).wait_send()
                partial_rows(sim, lo, rows)

                @pl.when(has_above)
                def _():
                    up_copy(step + 1, sim, lo, rows).start()

        for lo in pieces(rows):
            @pl.when(has_above)
            def _():
                down_copy(step, sim, lo, rows).wait_recv()
            magnetic_last(step, sim, lo, rows)
            electric_rows(step, sim, last, lo, rows)
            if far:
                share_out(step, sim, 1, pl.ds(last, 1), lo, rows)
            if lo > 0:
                send(lo - rows)
        send(width_y - rows)

    def bottom_rows(step, sim, rows, far):
        @pl.when(has_below)
        def _():
            for lo in pieces(rows):
                down_copy(step, sim, lo, rows).wait_send()
        if far:
            electric_rows(step, sim, 0, 0, width_y, True)
        for lo in pieces(rows):
            @pl.when(has_below)
            def _():
                up_copy(step, sim, lo, rows).wait_recv()
            if far:
                electric_first(step, sim, lo, rows)
            else:
                electric_rows(step, sim, 0, lo, rows)
            if far:
                share_out(step, sim, 1, pl.ds(0, 1), lo, rows)

            @pl.when(jnp.logical_and(has_below, step < steps - 1))
            def _():
                down_copy(step + 1, sim, lo, rows).start()

    lax.fori_loop(1, slabs, take_tiles, 0)
    await_all(port_ready, port_devices - 1 - port)
    split_tiles()
    place_tiles(jnp.where(top_is_far, last, 0))

    def one_step(step, carry):
        for sim in range(2):
            def far_side():
                def odd():
                    top_rows(step, sim, FAR_ROWS, True)

                def even():
                    bottom_rows(step, sim, FAR_ROWS, True)

                by_side(odd, even)

            def near_side():
                if sim == 0:
                    @pl.when(step == 0)
                    def _():
                        lax.fori_loop(0, last, place_rest, 0)
                for layer in range(1, last):
                    electric_rows(step, sim, layer, 0, width_y)

                def odd():
                    bottom_rows(step, sim, width_y, False)
                    share_out(step, sim, 0, pl.ds(0, last), 0, width_y)

                def even():
                    top_rows(step, sim, width_y, False)
                    share_out(step, sim, 0, pl.ds(1, last), 0, width_y)

                by_side(odd, even)

            def one_side(turn, carry):
                far_turn = turn == jnp.where(step == 0, 0, 1)
                pl.when(far_turn)(far_side)
                pl.when(jnp.logical_not(far_turn))(near_side)
                return carry

            lax.fori_loop(0, 2, one_side, 0)

            @pl.when(step < steps - 1)
            def _():
                magnetic_inside(sim)
        return carry

    lax.fori_loop(0, steps, one_step, 0)

    def faces_gone(up_rows):
        @pl.when(has_above)
        def _():
            for sim in range(2):
                for lo in pieces(up_rows):
                    up_copy(0, sim, lo, up_rows).wait_send()

    by_side(lambda: faces_gone(FAR_ROWS), lambda: faces_gone(width_y))
    lax.fori_loop(1, slabs, tiles_gone, 0)

    def add_shares(parts):
        for k in range(1, port_devices):
            for group, layers in enumerate(parts):
                share_copy(k, group, layers).wait_recv()
        total = summed[:, share_span(port)]
        for k in range(1, port_devices):
            total = total + shares[k]
        result[...] = total * (1.0 / math.sqrt(ports_ref.shape[1] * steps))
        for k in range(1, port_devices):
            for group, layers in enumerate(parts):
                share_copy(k, group, layers).wait_send()

    by_side(
        lambda: add_shares((pl.ds(0, last), pl.ds(last, 1))),
        lambda: add_shares((pl.ds(1, last), pl.ds(0, 1))))


def store_kernel(elec, magn, total, out_fields, out_sens, sem):
    rows = out_fields.shape[4]
    copies = [pltpu.make_async_copy(total, out_sens, sem.at[0])]
    for sim in range(2):
        for comp in range(3):
            copies.append(pltpu.make_async_copy(
                elec.at[sim, comp, :, pl.ds(0, rows)], out_fields.at[sim, 0, comp], sem.at[len(copies)]))
            copies.append(pltpu.make_async_copy(
                magn.at[sim, comp, :, pl.ds(PAD, rows)], out_fields.at[sim, 0, 3 + comp], sem.at[len(copies)]))
    for copy in copies:
        copy.start()
    for copy in copies:
        copy.wait()


def solution(mesh):
    slabs, port_devices = mesh.shape["space"], mesh.shape["port"]

    def local(fields, inv_eps, tensor_tiles, tile_index, ports, waves):
        assert fields.shape[1] == 1
        width_x, width_y, width_z = fields.shape[3:]
        steps = waves.shape[2]
        slots = tile_index.shape[2]
        owner_rows = tensor_tiles.shape[2]
        share_rows = width_y // port_devices
        far_pieces = width_y // FAR_ROWS
        f32 = jnp.float32
        dma = pltpu.SemaphoreType.DMA
        held = pl.BlockSpec(memory_space=pltpu.HBM)
        onchip = pl.BlockSpec(memory_space=pltpu.VMEM)
        anywhere = pl.BlockSpec(memory_space=pl.ANY)
        state = pl.pallas_call(
            functools.partial(kernel, slabs, port_devices),
            out_shape=(
                pltpu.VMEM((2, 3, width_x, width_y + PAD, width_z), f32),
                pltpu.VMEM((2, 3, width_x, width_y + PAD, width_z), f32),
                pltpu.VMEM((width_x, share_rows, width_z), f32),
            ),
            in_specs=[held] * 6,
            out_specs=(onchip, onchip, onchip),
            scratch_shapes=[
                pltpu.SMEM(ports.shape, jnp.int32),
                pltpu.SMEM(waves.shape, f32),
                pltpu.VMEM((steps, 2, 2, width_y, width_z), f32),
                pltpu.VMEM((steps, 2, 2, width_y, width_z), f32),
                pltpu.VMEM((2, 2, width_y, width_z), f32),
                pltpu.VMEM((6, 3 * slabs * slots, width_z), jnp.bfloat16),
                pltpu.VMEM((6, width_x, width_y, width_z), f32),
                pltpu.VMEM((3, width_x, width_y, width_z), f32),
                pltpu.VMEM((slabs * owner_rows, width_z), f32),
                pltpu.VMEM((slots, slabs), jnp.int32),
                pltpu.VMEM((width_x * width_y, 3 * slabs * slots), jnp.bfloat16),
                pltpu.VMEM((width_x * width_y, width_z), f32),
                pltpu.VMEM((width_x, width_y, width_z), f32),
                pltpu.VMEM((port_devices, width_x, share_rows, width_z), f32),
                dma((7,)),
                dma((slabs,)),
                dma((slabs,)),
                dma((2, far_pieces)),
                dma((steps, 2, far_pieces)),
                dma((2, far_pieces)),
                dma((steps, 2, far_pieces)),
                dma((port_devices, 2)),
                dma((port_devices, 2)),
                pltpu.SemaphoreType.REGULAR((GROUPS,)),
                pltpu.SemaphoreType.REGULAR,
            ],
            compiler_params=pltpu.CompilerParams(
                collective_id=0, has_side_effects=True, vmem_limit_bytes=40 * 1024 * 1024),
            name="window",
        )(*[pltpu.with_memory_space_constraint(x, pltpu.HBM) for x in (ports, waves, fields, inv_eps, tensor_tiles, tile_index.transpose(0, 2, 1))])
        return pl.pallas_call(
            store_kernel,
            out_shape=(
                jax.ShapeDtypeStruct(fields.shape, f32),
                jax.ShapeDtypeStruct((width_x, share_rows, width_z), f32),
            ),
            in_specs=[anywhere] * 3,
            out_specs=(anywhere, anywhere),
            scratch_shapes=[dma((13,))],
            compiler_params=pltpu.CompilerParams(vmem_limit_bytes=4 * 1024 * 1024),
            name="store",
        )(*[pltpu.with_memory_space_constraint(x, pltpu.VMEM) for x in state])

    in_specs = (
        P(None, "port", None, "space", None, None),
        P(None, "space", None, None),
        P("space", None, None, None),
        P("space", None, None),
        P(),
        P(None, "port", None),
    )
    out_specs = (P(None, "port", None, "space", None, None), P("space", "port", None))
    return jax.shard_map(local, mesh=mesh, in_specs=in_specs, out_specs=out_specs, check_vma=False)
```

```python
import functools
import math

import jax
import jax.numpy as jnp
from jax import lax
from jax.experimental import pallas as pl
from jax.experimental.pallas import tpu as pltpu
from jax.sharding import PartitionSpec as P

MESH = pl.DeviceIdType.MESH
magnetic_coef = 0.5
PAD = 8
ROWS = 8
FAR_ROWS = 16
GROUPS = 4


def kernel(
    slabs, port_devices, ports_in, waves_in, fields, inv_eps, tiles, tile_index,
    elec, magn, result,
    ports_ref, waves_ref, face_up, face_down, partial, pieces_ref, tensor, bulk, arrived, index, onehot, live, summed,
    shares, load_sem, tile_send, tile_recv, up_send, up_recv, down_send, down_recv,
    share_send, share_recv, ready, port_ready,
):
    me = lax.axis_index("space")
    port = lax.axis_index("port")
    width_x, width_y, width_z = inv_eps.shape[1:]
    steps = waves_ref.shape[2]
    last = width_x - 1
    owner_rows = tiles.shape[2]
    slots = owner_rows // 6
    share_rows = width_y // port_devices
    has_below = me > 0
    has_above = me < slabs - 1
    above = jnp.minimum(me + 1, slabs - 1)
    below = jnp.maximum(me - 1, 0)

    def owner_span(owner):
        return pl.ds(pl.multiple_of(owner * owner_rows, 8), owner_rows)

    barrier = pltpu.get_barrier_semaphore()

    size = slabs // GROUPS
    group = me // size

    def signal(semaphore, slab, along):
        pl.semaphore_signal(semaphore, inc=1, device_id=(slab, along), device_id_type=MESH)

    def await_all(semaphore, count):
        @pl.when(count > 0)
        def _():
            pl.semaphore_wait(semaphore, count)

    def each(low, high, act):
        def body(slab, carry):
            act(slab)
            return carry
        lax.fori_loop(low, high, body, 0)

    each(me + 1, slabs, lambda slab: signal(barrier, slab, port))
    each(port + 1, port_devices, lambda along: signal(barrier, me, along))

    loads = [
        pltpu.make_async_copy(fields.at[:, 0, pl.ds(0, 3)], elec.at[:, :, :, pl.ds(0, width_y)], load_sem.at[0]),
        pltpu.make_async_copy(fields.at[:, 0, pl.ds(3, 3)], magn.at[:, :, :, pl.ds(PAD, width_y)], load_sem.at[1]),
        pltpu.make_async_copy(inv_eps, bulk, load_sem.at[2]),
        pltpu.make_async_copy(tile_index.at[0], index, load_sem.at[3]),
        pltpu.make_async_copy(tiles.at[0, me], arrived.at[owner_span(me)], load_sem.at[4]),
        pltpu.make_async_copy(ports_in, ports_ref, load_sem.at[5]),
        pltpu.make_async_copy(waves_in, waves_ref, load_sem.at[6]),
    ]
    for load in (loads[3], loads[5], loads[6], loads[0], loads[1], loads[2], loads[4]):
        load.start()

    def up_copy(step, sim, lo, rows):
        span, k = pl.ds(lo, rows), lo // rows
        return pltpu.make_async_remote_copy(
            partial.at[sim, :, span], face_down.at[step, sim, :, span],
            up_send.at[sim, k], up_recv.at[step, sim, k], device_id=(above, port), device_id_type=MESH)

    def down_copy(step, sim, lo, rows):
        span, k = pl.ds(lo, rows), lo // rows
        return pltpu.make_async_remote_copy(
            elec.at[sim, pl.ds(1, 2), 0, span], face_up.at[step, sim, :, span],
            down_send.at[sim, k], down_recv.at[step, sim, k], device_id=(below, port), device_id_type=MESH)

    top_is_far = lax.rem(me, 2) == 1

    def by_side(odd, even):
        pl.when(top_is_far)(odd)
        pl.when(jnp.logical_not(top_is_far))(even)

    def pieces(rows):
        return range(0, width_y, rows)

    def tile_copy(k):
        target = lax.rem(me + k, slabs)
        return pltpu.make_async_remote_copy(
            tiles.at[0, target], arrived.at[owner_span(me)],
            tile_send.at[k], tile_recv.at[k], device_id=(target, port), device_id_type=MESH)

    def send_tile(slab):
        tile_copy(lax.rem(slab - me + slabs, slabs)).start()

    await_all(barrier, me + port)
    each(0, me, lambda slab: signal(ready.at[group - slab // size], slab, port))
    each(0, port, lambda along: signal(port_ready, me, along))
    each(0, me, send_tile)

    for offset in range(1):
        ahead = group + offset

        @pl.when(ahead < GROUPS)
        def _():
            low = jnp.maximum(ahead * size, me + 1)
            high = (ahead + 1) * size
            await_all(ready.at[offset], high - low)
            each(low, high, send_tile)

    zero_rows = jnp.zeros((PAD, width_z), jnp.float32)
    for sim in range(2):
        for comp in range(3):
            for layer in range(width_x):
                elec[sim, comp, layer, pl.ds(width_y, PAD)] = zero_rows
                magn[sim, comp, layer, pl.ds(0, PAD)] = zero_rows
    zero_plane = jnp.zeros((width_y, width_z), jnp.float32)

    @pl.when(me == 0)
    def _():
        def clear(step, carry):
            for sim in range(2):
                for comp in range(2):
                    face_down[step, sim, comp] = zero_plane
            return carry
        lax.fori_loop(0, steps, clear, 0)

    @pl.when(me == slabs - 1)
    def _():
        def clear(step, carry):
            for sim in range(2):
                for comp in range(2):
                    face_up[step, sim, comp] = zero_plane
            return carry
        lax.fori_loop(0, steps, clear, 0)

    for layer in range(width_x):
        summed[layer] = zero_plane

    columns = width_x * width_y
    loads[3].wait()
    spots_down = lax.broadcasted_iota(jnp.int32, (columns, slabs), 0)
    for k in range(slots):
        marks = jnp.where(index[k : k + 1, :] == spots_down, 1.0, 0.0).astype(jnp.bfloat16)
        for part in range(3):
            onehot[:, (part * slots + k) * slabs : (part * slots + k + 1) * slabs] = marks
    live[...] = jnp.dot(
        onehot[...], jnp.ones((3 * slabs * slots, width_z), jnp.bfloat16), preferred_element_type=jnp.float32)

    lane = lax.broadcasted_iota(jnp.int32, (ROWS, width_z), 1)
    row = lax.broadcasted_iota(jnp.int32, (ROWS, width_z), 0)
    cell_ids = row * width_z + lane
    not_last = lane < width_z - 1
    not_first = lane > 0
    plane = width_y * width_z
    loads[5].wait()
    loads[6].wait()
    source_cell = [ports_ref[sim, port] - me * (width_x * plane) for sim in range(2)]

    def next_z(values):
        return jnp.where(not_last, pltpu.roll(values, width_z - 1, 1), 0.0)

    def prev_z(values):
        return jnp.where(not_first, pltpu.roll(values, 1, 1), 0.0)

    def magnetic_rows(sim, layer, lo, rows):
        for y in range(lo, lo + rows, ROWS):
            at, nxt, hat = pl.ds(y, ROWS), pl.ds(y + 1, ROWS), pl.ds(PAD + y, ROWS)
            ey = elec[sim, 1, layer, at]
            ez = elec[sim, 2, layer, at]
            magn[sim, 0, layer, hat] = magn[sim, 0, layer, hat] - magnetic_coef * (
                elec[sim, 2, layer, nxt] - ez - (next_z(ey) - ey))
            if layer < last:
                ex = elec[sim, 0, layer, at]
                magn[sim, 1, layer, hat] = magn[sim, 1, layer, hat] - magnetic_coef * (
                    next_z(ex) - ex - (elec[sim, 2, layer + 1, at] - ez))
                magn[sim, 2, layer, hat] = magn[sim, 2, layer, hat] - magnetic_coef * (
                    elec[sim, 1, layer + 1, at] - ey - (elec[sim, 0, layer, nxt] - ex))

    def magnetic_last(step, sim, lo, rows):
        for y in range(lo, lo + rows, ROWS):
            at, hat = pl.ds(y, ROWS), pl.ds(PAD + y, ROWS)
            magn[sim, 1, last, hat] = partial[sim, 0, at] + magnetic_coef * face_up[step, sim, 1, at]
            magn[sim, 2, last, hat] = partial[sim, 1, at] - magnetic_coef * face_up[step, sim, 0, at]

    def partial_rows(sim, lo, rows):
        for y in range(lo, lo + rows, ROWS):
            at, nxt, hat = pl.ds(y, ROWS), pl.ds(y + 1, ROWS), pl.ds(PAD + y, ROWS)
            ex = elec[sim, 0, last, at]
            partial[sim, 0, at] = magn[sim, 1, last, hat] - magnetic_coef * (
                next_z(ex) - ex + elec[sim, 2, last, at])
            partial[sim, 1, at] = magn[sim, 2, last, hat] + magnetic_coef * (
                elec[sim, 1, last, at] + (elec[sim, 0, last, nxt] - ex))

    def electric_first(step, sim, lo, rows):
        for y in range(lo, lo + rows, ROWS):
            at = pl.ds(y, ROWS)
            hy, hz = face_down[step, sim, 0, at], face_down[step, sim, 1, at]
            xy, xz, yz = tensor[3, 0, at], tensor[4, 0, at], tensor[5, 0, at]
            ex = elec[sim, 0, 0, at] + (xy * hz - xz * hy)
            ey = elec[sim, 1, 0, at] + (tensor[1, 0, at] * hz - yz * hy)
            ez = elec[sim, 2, 0, at] + (yz * hz - tensor[2, 0, at] * hy)
            elec[sim, 0, 0, at] = ex
            elec[sim, 1, 0, at] = ey
            elec[sim, 2, 0, at] = ez
            if sim == 1:
                summed[0, at] = summed[0, at] + (
                    elec[0, 0, 0, at] * ex + elec[0, 1, 0, at] * ey + elec[0, 2, 0, at] * ez)

    halo_coef = jnp.where(has_below, magnetic_coef, 0.0).astype(jnp.float32)

    def electric_rows(step, sim, layer, lo, rows, ahead=False):
        pulse = waves_ref[sim, 0, step]
        for y in range(lo, lo + rows, ROWS):
            at, hat, prv = pl.ds(y, ROWS), pl.ds(PAD + y, ROWS), pl.ds(PAD + y - 1, ROWS)
            hx = magn[sim, 0, layer, hat]
            hy = magn[sim, 1, layer, hat]
            hz = magn[sim, 2, layer, hat]
            ex = elec[sim, 0, layer, at]
            ey = elec[sim, 1, layer, at]
            ez = elec[sim, 2, layer, at]
            if layer > 0:
                hy_down, hz_down = magn[sim, 1, layer - 1, hat], magn[sim, 2, layer - 1, hat]
            elif ahead:
                hy_down, hz_down = halo_coef * ez, -halo_coef * ey
            else:
                hy_down = face_down[step, sim, 0, at] + halo_coef * ez
                hz_down = face_down[step, sim, 1, at] - halo_coef * ey
            cx = hz - magn[sim, 2, layer, prv] - (hy - prev_z(hy))
            cy = hx - prev_z(hx) - (hz - hz_down)
            cz = hy - hy_down - (hx - magn[sim, 0, layer, prv])
            xy, xz, yz = tensor[3, layer, at], tensor[4, layer, at], tensor[5, layer, at]
            ex = ex + (tensor[0, layer, at] * cx + xy * cy + xz * cz)
            ey = ey + (xy * cx + tensor[1, layer, at] * cy + yz * cz)
            ez = ez + (xz * cx + yz * cy + tensor[2, layer, at] * cz)
            here = source_cell[sim] - (layer * plane + y * width_z)
            ez = ez + jnp.where(cell_ids == here, pulse, 0.0)
            elec[sim, 0, layer, at] = ex
            elec[sim, 1, layer, at] = ey
            elec[sim, 2, layer, at] = ez
            if sim == 1 and not ahead:
                summed[layer, at] = summed[layer, at] + (
                    elec[0, 0, layer, at] * ex + elec[0, 1, layer, at] * ey + elec[0, 2, layer, at] * ez)

    loads[0].wait()
    loads[1].wait()
    for sim in range(2):
        partial_rows(sim, 0, width_y)

    for offset in range(1, GROUPS):
        ahead = group + offset

        @pl.when(ahead < GROUPS)
        def _():
            low = jnp.maximum(ahead * size, me + 1)
            high = (ahead + 1) * size
            await_all(ready.at[offset], high - low)
            each(low, high, send_tile)

    def first_faces(up_rows, down_rows):
        @pl.when(has_above)
        def _():
            for sim in range(2):
                for lo in pieces(up_rows):
                    up_copy(0, sim, lo, up_rows).start()

        @pl.when(has_below)
        def _():
            for sim in range(2):
                for lo in pieces(down_rows):
                    down_copy(0, sim, lo, down_rows).start()

    by_side(lambda: first_faces(FAR_ROWS, width_y), lambda: first_faces(width_y, FAR_ROWS))

    def magnetic_inside(sim):
        for layer in range(width_x):
            magnetic_rows(sim, layer, 0, width_y)

    for sim in range(2):
        magnetic_inside(sim)
    loads[2].wait()
    loads[4].wait()

    def take_tiles(k, carry):
        tile_copy(k).wait_recv()
        return carry

    def tiles_gone(k, carry):
        tile_copy(k).wait_send()
        return carry

    def split_tiles():
        for entry in range(6):
            block = jnp.concatenate(
                [arrived[pl.ds(6 * k + entry, slabs, stride=owner_rows), :] for k in range(slots)], 0)
            high = block.astype(jnp.bfloat16)
            rest = block - high.astype(jnp.float32)
            middle = rest.astype(jnp.bfloat16)
            low = (rest - middle.astype(jnp.float32)).astype(jnp.bfloat16)
            for part, values in enumerate((high, middle, low)):
                pieces_ref[entry, part * slots * slabs : (part + 1) * slots * slabs] = values

    def place_tiles(layer):
        rows = pl.ds(pl.multiple_of(layer * width_y, 16), width_y)
        spots = onehot[rows, :]
        taken = live[rows, :] > 0.5
        for entry in range(6):
            placed = jnp.dot(spots, pieces_ref[entry], preferred_element_type=jnp.float32)
            tensor[entry, layer] = jnp.where(taken, placed, bulk[entry, layer] if entry < 3 else 0.0)

    def place_rest(k, carry):
        place_tiles(k + jnp.where(top_is_far, 0, 1))
        return carry

    def share_span(device):
        return pl.ds(pl.multiple_of(device * share_rows, 8), share_rows)

    def share_copy(k, group, layers):
        target = lax.rem(port + k, port_devices)
        return pltpu.make_async_remote_copy(
            summed.at[layers, share_span(target)], shares.at[k, layers],
            share_send.at[k, group], share_recv.at[k, group], device_id=(me, target), device_id_type=MESH)

    def share_out(step, sim, group, layers, lo, rows):
        if sim == 1:
            for k in range(1, port_devices):
                end = (lax.rem(port + k, port_devices) + 1) * share_rows

                @pl.when((step == steps - 1) & (end > lo) & (end <= lo + rows))
                def _():
                    share_copy(k, group, layers).start()

    def top_rows(step, sim, rows, far):
        def send(lo):
            @pl.when(step < steps - 1)
            def _():
                partial_rows(sim, lo, rows)

                @pl.when(has_above)
                def _():
                    up_copy(step + 1, sim, lo, rows).start()

        @pl.when(jnp.logical_and(has_above, step < steps - 1))
        def _():
            for lo in pieces(rows):
                up_copy(step, sim, lo, rows).wait_send()

        for lo in pieces(rows):
            @pl.when(has_above)
            def _():
                down_copy(step, sim, lo, rows).wait_recv()
            magnetic_last(step, sim, lo, rows)
            electric_rows(step, sim, last, lo, rows)
            if far:
                share_out(step, sim, 1, pl.ds(last, 1), lo, rows)
            if lo > 0:
                send(lo - rows)
        send(width_y - rows)

    def bottom_rows(step, sim, rows, far):
        @pl.when(has_below)
        def _():
            for lo in pieces(rows):
                down_copy(step, sim, lo, rows).wait_send()
        if far:
            electric_rows(step, sim, 0, 0, width_y, True)
        for lo in pieces(rows):
            @pl.when(has_below)
            def _():
                up_copy(step, sim, lo, rows).wait_recv()
            if far:
                electric_first(step, sim, lo, rows)
            else:
                electric_rows(step, sim, 0, lo, rows)
            if far:
                share_out(step, sim, 1, pl.ds(0, 1), lo, rows)

            @pl.when(jnp.logical_and(has_below, step < steps - 1))
            def _():
                down_copy(step + 1, sim, lo, rows).start()

    lax.fori_loop(1, slabs, take_tiles, 0)
    await_all(port_ready, port_devices - 1 - port)
    split_tiles()
    place_tiles(jnp.where(top_is_far, last, 0))

    def one_step(step, carry):
        for sim in range(2):
            def far_side():
                def odd():
                    top_rows(step, sim, FAR_ROWS, True)

                def even():
                    bottom_rows(step, sim, FAR_ROWS, True)

                by_side(odd, even)

            def near_side():
                if sim == 0:
                    @pl.when(step == 0)
                    def _():
                        lax.fori_loop(0, last, place_rest, 0)
                for layer in range(1, last):
                    electric_rows(step, sim, layer, 0, width_y)

                def odd():
                    bottom_rows(step, sim, width_y, False)
                    share_out(step, sim, 0, pl.ds(0, last), 0, width_y)

                def even():
                    top_rows(step, sim, width_y, False)
                    share_out(step, sim, 0, pl.ds(1, last), 0, width_y)

                by_side(odd, even)

            def one_side(turn, carry):
                far_turn = turn == jnp.where(step == 0, 0, 1)
                pl.when(far_turn)(far_side)
                pl.when(jnp.logical_not(far_turn))(near_side)
                return carry

            lax.fori_loop(0, 2, one_side, 0)

            @pl.when(step < steps - 1)
            def _():
                magnetic_inside(sim)
        return carry

    lax.fori_loop(0, steps, one_step, 0)

    def faces_gone(up_rows):
        @pl.when(has_above)
        def _():
            for sim in range(2):
                for lo in pieces(up_rows):
                    up_copy(0, sim, lo, up_rows).wait_send()

    by_side(lambda: faces_gone(FAR_ROWS), lambda: faces_gone(width_y))
    lax.fori_loop(1, slabs, tiles_gone, 0)

    def add_shares(parts):
        for k in range(1, port_devices):
            for group, layers in enumerate(parts):
                share_copy(k, group, layers).wait_recv()
        total = summed[:, share_span(port)]
        for k in range(1, port_devices):
            total = total + shares[k]
        result[...] = total * (1.0 / math.sqrt(ports_ref.shape[1] * steps))
        for k in range(1, port_devices):
            for group, layers in enumerate(parts):
                share_copy(k, group, layers).wait_send()

    by_side(
        lambda: add_shares((pl.ds(0, last), pl.ds(last, 1))),
        lambda: add_shares((pl.ds(1, last), pl.ds(0, 1))))


def store_kernel(elec, magn, total, out_fields, out_sens, sem):
    rows = out_fields.shape[4]
    copies = [pltpu.make_async_copy(total, out_sens, sem.at[0])]
    for sim in range(2):
        for comp in range(3):
            copies.append(pltpu.make_async_copy(
                elec.at[sim, comp, :, pl.ds(0, rows)], out_fields.at[sim, 0, comp], sem.at[len(copies)]))
            copies.append(pltpu.make_async_copy(
                magn.at[sim, comp, :, pl.ds(PAD, rows)], out_fields.at[sim, 0, 3 + comp], sem.at[len(copies)]))
    for copy in copies:
        copy.start()
    for copy in copies:
        copy.wait()


def solution(mesh):
    slabs, port_devices = mesh.shape["space"], mesh.shape["port"]

    def local(fields, inv_eps, tensor_tiles, tile_index, ports, waves):
        assert fields.shape[1] == 1
        width_x, width_y, width_z = fields.shape[3:]
        steps = waves.shape[2]
        slots = tile_index.shape[2]
        owner_rows = tensor_tiles.shape[2]
        share_rows = width_y // port_devices
        far_pieces = width_y // FAR_ROWS
        f32 = jnp.float32
        dma = pltpu.SemaphoreType.DMA
        held = pl.BlockSpec(memory_space=pltpu.HBM)
        onchip = pl.BlockSpec(memory_space=pltpu.VMEM)
        anywhere = pl.BlockSpec(memory_space=pl.ANY)
        state = pl.pallas_call(
            functools.partial(kernel, slabs, port_devices),
            out_shape=(
                pltpu.VMEM((2, 3, width_x, width_y + PAD, width_z), f32),
                pltpu.VMEM((2, 3, width_x, width_y + PAD, width_z), f32),
                pltpu.VMEM((width_x, share_rows, width_z), f32),
            ),
            in_specs=[held] * 6,
            out_specs=(onchip, onchip, onchip),
            scratch_shapes=[
                pltpu.SMEM(ports.shape, jnp.int32),
                pltpu.SMEM(waves.shape, f32),
                pltpu.VMEM((steps, 2, 2, width_y, width_z), f32),
                pltpu.VMEM((steps, 2, 2, width_y, width_z), f32),
                pltpu.VMEM((2, 2, width_y, width_z), f32),
                pltpu.VMEM((6, 3 * slabs * slots, width_z), jnp.bfloat16),
                pltpu.VMEM((6, width_x, width_y, width_z), f32),
                pltpu.VMEM((3, width_x, width_y, width_z), f32),
                pltpu.VMEM((slabs * owner_rows, width_z), f32),
                pltpu.VMEM((slots, slabs), jnp.int32),
                pltpu.VMEM((width_x * width_y, 3 * slabs * slots), jnp.bfloat16),
                pltpu.VMEM((width_x * width_y, width_z), f32),
                pltpu.VMEM((width_x, width_y, width_z), f32),
                pltpu.VMEM((port_devices, width_x, share_rows, width_z), f32),
                dma((7,)),
                dma((slabs,)),
                dma((slabs,)),
                dma((2, far_pieces)),
                dma((steps, 2, far_pieces)),
                dma((2, far_pieces)),
                dma((steps, 2, far_pieces)),
                dma((port_devices, 2)),
                dma((port_devices, 2)),
                pltpu.SemaphoreType.REGULAR((GROUPS,)),
                pltpu.SemaphoreType.REGULAR,
            ],
            compiler_params=pltpu.CompilerParams(
                collective_id=0, has_side_effects=True, vmem_limit_bytes=40 * 1024 * 1024),
            name="window",
        )(*[pltpu.with_memory_space_constraint(x, pltpu.HBM) for x in (ports, waves, fields, inv_eps, tensor_tiles, tile_index.transpose(0, 2, 1))])
        return pl.pallas_call(
            store_kernel,
            out_shape=(
                jax.ShapeDtypeStruct(fields.shape, f32),
                jax.ShapeDtypeStruct((width_x, share_rows, width_z), f32),
            ),
            in_specs=[anywhere] * 3,
            out_specs=(anywhere, anywhere),
            scratch_shapes=[dma((13,))],
            compiler_params=pltpu.CompilerParams(vmem_limit_bytes=4 * 1024 * 1024),
            name="store",
        )(*[pltpu.with_memory_space_constraint(x, pltpu.VMEM) for x in state])

    in_specs = (
        P(None, "port", None, "space", None, None),
        P(None, "space", None, None),
        P("space", None, None, None),
        P("space", None, None),
        P(),
        P(None, "port", None),
    )
    out_specs = (P(None, "port", None, "space", None, None), P("space", "port", None))
    return jax.shard_map(local, mesh=mesh, in_specs=in_specs, out_specs=out_specs, check_vma=False)
```

```python
import functools
import math

import jax
import jax.numpy as jnp
from jax import lax
from jax.experimental import pallas as pl
from jax.experimental.pallas import tpu as pltpu
from jax.sharding import PartitionSpec as P

MESH = pl.DeviceIdType.MESH
magnetic_coef = 0.5
PAD = 8
ROWS = 16
FAR_ROWS = 16
GROUPS = 4


def kernel(
    slabs, port_devices, ports_in, waves_in, fields, inv_eps, tiles, tile_index,
    elec, magn, result,
    ports_ref, waves_ref, face_up, face_down, partial, pieces_ref, tensor, bulk, arrived, index, onehot, live, summed,
    shares, load_sem, tile_send, tile_recv, up_send, up_recv, down_send, down_recv,
    share_send, share_recv, ready, port_ready,
):
    me = lax.axis_index("space")
    port = lax.axis_index("port")
    width_x, width_y, width_z = inv_eps.shape[1:]
    steps = waves_ref.shape[2]
    last = width_x - 1
    owner_rows = tiles.shape[2]
    slots = owner_rows // 6
    share_rows = width_y // port_devices
    has_below = me > 0
    has_above = me < slabs - 1
    above = jnp.minimum(me + 1, slabs - 1)
    below = jnp.maximum(me - 1, 0)

    def owner_span(owner):
        return pl.ds(pl.multiple_of(owner * owner_rows, 8), owner_rows)

    barrier = pltpu.get_barrier_semaphore()

    size = slabs // GROUPS
    group = me // size

    def signal(semaphore, slab, along):
        pl.semaphore_signal(semaphore, inc=1, device_id=(slab, along), device_id_type=MESH)

    def await_all(semaphore, count):
        @pl.when(count > 0)
        def _():
            pl.semaphore_wait(semaphore, count)

    def each(low, high, act):
        def body(slab, carry):
            act(slab)
            return carry
        lax.fori_loop(low, high, body, 0)

    each(me + 1, slabs, lambda slab: signal(barrier, slab, port))
    each(port + 1, port_devices, lambda along: signal(barrier, me, along))

    loads = [
        pltpu.make_async_copy(fields.at[:, 0, pl.ds(0, 3)], elec.at[:, :, :, pl.ds(0, width_y)], load_sem.at[0]),
        pltpu.make_async_copy(fields.at[:, 0, pl.ds(3, 3)], magn.at[:, :, :, pl.ds(PAD, width_y)], load_sem.at[1]),
        pltpu.make_async_copy(inv_eps, bulk, load_sem.at[2]),
        pltpu.make_async_copy(tile_index.at[0], index, load_sem.at[3]),
        pltpu.make_async_copy(tiles.at[0, me], arrived.at[owner_span(me)], load_sem.at[4]),
        pltpu.make_async_copy(ports_in, ports_ref, load_sem.at[5]),
        pltpu.make_async_copy(waves_in, waves_ref, load_sem.at[6]),
    ]
    for load in (loads[3], loads[5], loads[6], loads[0], loads[1], loads[2], loads[4]):
        load.start()

    def up_copy(step, sim, lo, rows):
        span, k = pl.ds(lo, rows), lo // rows
        return pltpu.make_async_remote_copy(
            partial.at[sim, :, span], face_down.at[step, sim, :, span],
            up_send.at[sim, k], up_recv.at[step, sim, k], device_id=(above, port), device_id_type=MESH)

    def down_copy(step, sim, lo, rows):
        span, k = pl.ds(lo, rows), lo // rows
        return pltpu.make_async_remote_copy(
            elec.at[sim, pl.ds(1, 2), 0, span], face_up.at[step, sim, :, span],
            down_send.at[sim, k], down_recv.at[step, sim, k], device_id=(below, port), device_id_type=MESH)

    top_is_far = lax.rem(me, 2) == 1

    def by_side(odd, even):
        pl.when(top_is_far)(odd)
        pl.when(jnp.logical_not(top_is_far))(even)

    def pieces(rows):
        return range(0, width_y, rows)

    def tile_copy(k):
        target = lax.rem(me + k, slabs)
        return pltpu.make_async_remote_copy(
            tiles.at[0, target], arrived.at[owner_span(me)],
            tile_send.at[k], tile_recv.at[k], device_id=(target, port), device_id_type=MESH)

    def send_tile(slab):
        tile_copy(lax.rem(slab - me + slabs, slabs)).start()

    await_all(barrier, me + port)
    each(0, me, lambda slab: signal(ready.at[group - slab // size], slab, port))
    each(0, port, lambda along: signal(port_ready, me, along))
    each(0, me, send_tile)

    for offset in range(1):
        ahead = group + offset

        @pl.when(ahead < GROUPS)
        def _():
            low = jnp.maximum(ahead * size, me + 1)
            high = (ahead + 1) * size
            await_all(ready.at[offset], high - low)
            each(low, high, send_tile)

    zero_rows = jnp.zeros((PAD, width_z), jnp.float32)
    for sim in range(2):
        for comp in range(3):
            for layer in range(width_x):
                elec[sim, comp, layer, pl.ds(width_y, PAD)] = zero_rows
                magn[sim, comp, layer, pl.ds(0, PAD)] = zero_rows
    zero_plane = jnp.zeros((width_y, width_z), jnp.float32)

    @pl.when(me == 0)
    def _():
        def clear(step, carry):
            for sim in range(2):
                for comp in range(2):
                    face_down[step, sim, comp] = zero_plane
            return carry
        lax.fori_loop(0, steps, clear, 0)

    @pl.when(me == slabs - 1)
    def _():
        def clear(step, carry):
            for sim in range(2):
                for comp in range(2):
                    face_up[step, sim, comp] = zero_plane
            return carry
        lax.fori_loop(0, steps, clear, 0)

    for layer in range(width_x):
        summed[layer] = zero_plane

    columns = width_x * width_y
    loads[3].wait()
    spots_down = lax.broadcasted_iota(jnp.int32, (columns, slabs), 0)
    for k in range(slots):
        marks = jnp.where(index[k : k + 1, :] == spots_down, 1.0, 0.0).astype(jnp.bfloat16)
        for part in range(3):
            onehot[:, (part * slots + k) * slabs : (part * slots + k + 1) * slabs] = marks
    live[...] = jnp.dot(
        onehot[...], jnp.ones((3 * slabs * slots, width_z), jnp.bfloat16), preferred_element_type=jnp.float32)

    lane = lax.broadcasted_iota(jnp.int32, (ROWS, width_z), 1)
    row = lax.broadcasted_iota(jnp.int32, (ROWS, width_z), 0)
    cell_ids = row * width_z + lane
    not_last = lane < width_z - 1
    not_first = lane > 0
    plane = width_y * width_z
    loads[5].wait()
    loads[6].wait()
    source_cell = [ports_ref[sim, port] - me * (width_x * plane) for sim in range(2)]

    def next_z(values):
        return jnp.where(not_last, pltpu.roll(values, width_z - 1, 1), 0.0)

    def prev_z(values):
        return jnp.where(not_first, pltpu.roll(values, 1, 1), 0.0)

    def magnetic_rows(sim, layer, lo, rows):
        for y in range(lo, lo + rows, ROWS):
            at, nxt, hat = pl.ds(y, ROWS), pl.ds(y + 1, ROWS), pl.ds(PAD + y, ROWS)
            ey = elec[sim, 1, layer, at]
            ez = elec[sim, 2, layer, at]
            magn[sim, 0, layer, hat] = magn[sim, 0, layer, hat] - magnetic_coef * (
                elec[sim, 2, layer, nxt] - ez - (next_z(ey) - ey))
            if layer < last:
                ex = elec[sim, 0, layer, at]
                magn[sim, 1, layer, hat] = magn[sim, 1, layer, hat] - magnetic_coef * (
                    next_z(ex) - ex - (elec[sim, 2, layer + 1, at] - ez))
                magn[sim, 2, layer, hat] = magn[sim, 2, layer, hat] - magnetic_coef * (
                    elec[sim, 1, layer + 1, at] - ey - (elec[sim, 0, layer, nxt] - ex))

    def magnetic_last(step, sim, lo, rows):
        for y in range(lo, lo + rows, ROWS):
            at, hat = pl.ds(y, ROWS), pl.ds(PAD + y, ROWS)
            magn[sim, 1, last, hat] = partial[sim, 0, at] + magnetic_coef * face_up[step, sim, 1, at]
            magn[sim, 2, last, hat] = partial[sim, 1, at] - magnetic_coef * face_up[step, sim, 0, at]

    def partial_rows(sim, lo, rows):
        for y in range(lo, lo + rows, ROWS):
            at, nxt, hat = pl.ds(y, ROWS), pl.ds(y + 1, ROWS), pl.ds(PAD + y, ROWS)
            ex = elec[sim, 0, last, at]
            partial[sim, 0, at] = magn[sim, 1, last, hat] - magnetic_coef * (
                next_z(ex) - ex + elec[sim, 2, last, at])
            partial[sim, 1, at] = magn[sim, 2, last, hat] + magnetic_coef * (
                elec[sim, 1, last, at] + (elec[sim, 0, last, nxt] - ex))

    def electric_first(step, sim, lo, rows):
        for y in range(lo, lo + rows, ROWS):
            at = pl.ds(y, ROWS)
            hy, hz = face_down[step, sim, 0, at], face_down[step, sim, 1, at]
            xy, xz, yz = tensor[3, 0, at], tensor[4, 0, at], tensor[5, 0, at]
            ex = elec[sim, 0, 0, at] + (xy * hz - xz * hy)
            ey = elec[sim, 1, 0, at] + (tensor[1, 0, at] * hz - yz * hy)
            ez = elec[sim, 2, 0, at] + (yz * hz - tensor[2, 0, at] * hy)
            elec[sim, 0, 0, at] = ex
            elec[sim, 1, 0, at] = ey
            elec[sim, 2, 0, at] = ez
            if sim == 1:
                summed[0, at] = summed[0, at] + (
                    elec[0, 0, 0, at] * ex + elec[0, 1, 0, at] * ey + elec[0, 2, 0, at] * ez)

    halo_coef = jnp.where(has_below, magnetic_coef, 0.0).astype(jnp.float32)

    def electric_rows(step, sim, layer, lo, rows, ahead=False):
        pulse = waves_ref[sim, 0, step]
        for y in range(lo, lo + rows, ROWS):
            at, hat, prv = pl.ds(y, ROWS), pl.ds(PAD + y, ROWS), pl.ds(PAD + y - 1, ROWS)
            hx = magn[sim, 0, layer, hat]
            hy = magn[sim, 1, layer, hat]
            hz = magn[sim, 2, layer, hat]
            ex = elec[sim, 0, layer, at]
            ey = elec[sim, 1, layer, at]
            ez = elec[sim, 2, layer, at]
            if layer > 0:
                hy_down, hz_down = magn[sim, 1, layer - 1, hat], magn[sim, 2, layer - 1, hat]
            elif ahead:
                hy_down, hz_down = halo_coef * ez, -halo_coef * ey
            else:
                hy_down = face_down[step, sim, 0, at] + halo_coef * ez
                hz_down = face_down[step, sim, 1, at] - halo_coef * ey
            cx = hz - magn[sim, 2, layer, prv] - (hy - prev_z(hy))
            cy = hx - prev_z(hx) - (hz - hz_down)
            cz = hy - hy_down - (hx - magn[sim, 0, layer, prv])
            xy, xz, yz = tensor[3, layer, at], tensor[4, layer, at], tensor[5, layer, at]
            ex = ex + (tensor[0, layer, at] * cx + xy * cy + xz * cz)
            ey = ey + (xy * cx + tensor[1, layer, at] * cy + yz * cz)
            ez = ez + (xz * cx + yz * cy + tensor[2, layer, at] * cz)
            here = source_cell[sim] - (layer * plane + y * width_z)
            ez = ez + jnp.where(cell_ids == here, pulse, 0.0)
            elec[sim, 0, layer, at] = ex
            elec[sim, 1, layer, at] = ey
            elec[sim, 2, layer, at] = ez
            if sim == 1 and not ahead:
                summed[layer, at] = summed[layer, at] + (
                    elec[0, 0, layer, at] * ex + elec[0, 1, layer, at] * ey + elec[0, 2, layer, at] * ez)

    loads[0].wait()
    loads[1].wait()
    for sim in range(2):
        partial_rows(sim, 0, width_y)

    for offset in range(1, GROUPS):
        ahead = group + offset

        @pl.when(ahead < GROUPS)
        def _():
            low = jnp.maximum(ahead * size, me + 1)
            high = (ahead + 1) * size
            await_all(ready.at[offset], high - low)
            each(low, high, send_tile)

    def first_faces(up_rows, down_rows):
        @pl.when(has_above)
        def _():
            for sim in range(2):
                for lo in pieces(up_rows):
                    up_copy(0, sim, lo, up_rows).start()

        @pl.when(has_below)
        def _():
            for sim in range(2):
                for lo in pieces(down_rows):
                    down_copy(0, sim, lo, down_rows).start()

    by_side(lambda: first_faces(FAR_ROWS, width_y), lambda: first_faces(width_y, FAR_ROWS))

    def magnetic_inside(sim):
        for layer in range(width_x):
            magnetic_rows(sim, layer, 0, width_y)

    for sim in range(2):
        magnetic_inside(sim)
    loads[2].wait()
    loads[4].wait()

    def take_tiles(k, carry):
        tile_copy(k).wait_recv()
        return carry

    def tiles_gone(k, carry):
        tile_copy(k).wait_send()
        return carry

    def split_tiles():
        for entry in range(6):
            block = jnp.concatenate(
                [arrived[pl.ds(6 * k + entry, slabs, stride=owner_rows), :] for k in range(slots)], 0)
            high = block.astype(jnp.bfloat16)
            rest = block - high.astype(jnp.float32)
            middle = rest.astype(jnp.bfloat16)
            low = (rest - middle.astype(jnp.float32)).astype(jnp.bfloat16)
            for part, values in enumerate((high, middle, low)):
                pieces_ref[entry, part * slots * slabs : (part + 1) * slots * slabs] = values

    def place_tiles(layer):
        rows = pl.ds(pl.multiple_of(layer * width_y, 16), width_y)
        spots = onehot[rows, :]
        taken = live[rows, :] > 0.5
        for entry in range(6):
            placed = jnp.dot(spots, pieces_ref[entry], preferred_element_type=jnp.float32)
            tensor[entry, layer] = jnp.where(taken, placed, bulk[entry, layer] if entry < 3 else 0.0)

    def place_rest(k, carry):
        place_tiles(k + jnp.where(top_is_far, 0, 1))
        return carry

    def share_span(device):
        return pl.ds(pl.multiple_of(device * share_rows, 8), share_rows)

    def share_copy(k, group, layers):
        target = lax.rem(port + k, port_devices)
        return pltpu.make_async_remote_copy(
            summed.at[layers, share_span(target)], shares.at[k, layers],
            share_send.at[k, group], share_recv.at[k, group], device_id=(me, target), device_id_type=MESH)

    def share_out(step, sim, group, layers, lo, rows):
        if sim == 1:
            for k in range(1, port_devices):
                end = (lax.rem(port + k, port_devices) + 1) * share_rows

                @pl.when((step == steps - 1) & (end > lo) & (end <= lo + rows))
                def _():
                    share_copy(k, group, layers).start()

    def top_rows(step, sim, rows, far):
        def send(lo):
            @pl.when(step < steps - 1)
            def _():
                @pl.when(has_above)
                def _():
                    up_copy(step, sim, lo, rows).wait_send()
                partial_rows(sim, lo, rows)

                @pl.when(has_above)
                def _():
                    up_copy(step + 1, sim, lo, rows).start()

        for lo in pieces(rows):
            @pl.when(has_above)
            def _():
                down_copy(step, sim, lo, rows).wait_recv()
            magnetic_last(step, sim, lo, rows)
            electric_rows(step, sim, last, lo, rows)
            if far:
                share_out(step, sim, 1, pl.ds(last, 1), lo, rows)
            if lo > 0:
                send(lo - rows)
        send(width_y - rows)

    def bottom_rows(step, sim, rows, far):
        @pl.when(has_below)
        def _():
            for lo in pieces(rows):
                down_copy(step, sim, lo, rows).wait_send()
        if far:
            electric_rows(step, sim, 0, 0, width_y, True)
        for lo in pieces(rows):
            @pl.when(has_below)
            def _():
                up_copy(step, sim, lo, rows).wait_recv()
            if far:
                electric_first(step, sim, lo, rows)
            else:
                electric_rows(step, sim, 0, lo, rows)
            if far:
                share_out(step, sim, 1, pl.ds(0, 1), lo, rows)

            @pl.when(jnp.logical_and(has_below, step < steps - 1))
            def _():
                down_copy(step + 1, sim, lo, rows).start()

    lax.fori_loop(1, slabs, take_tiles, 0)
    await_all(port_ready, port_devices - 1 - port)
    split_tiles()
    place_tiles(jnp.where(top_is_far, last, 0))

    def one_step(step, carry):
        for sim in range(2):
            def far_side():
                def odd():
                    top_rows(step, sim, FAR_ROWS, True)

                def even():
                    bottom_rows(step, sim, FAR_ROWS, True)

                by_side(odd, even)

            def near_side():
                if sim == 0:
                    @pl.when(step == 0)
                    def _():
                        lax.fori_loop(0, last, place_rest, 0)
                for layer in range(1, last):
                    electric_rows(step, sim, layer, 0, width_y)

                def odd():
                    bottom_rows(step, sim, width_y, False)
                    share_out(step, sim, 0, pl.ds(0, last), 0, width_y)

                def even():
                    top_rows(step, sim, width_y, False)
                    share_out(step, sim, 0, pl.ds(1, last), 0, width_y)

                by_side(odd, even)

            def one_side(turn, carry):
                far_turn = turn == jnp.where(step == 0, 0, 1)
                pl.when(far_turn)(far_side)
                pl.when(jnp.logical_not(far_turn))(near_side)
                return carry

            lax.fori_loop(0, 2, one_side, 0)

            @pl.when(step < steps - 1)
            def _():
                magnetic_inside(sim)
        return carry

    lax.fori_loop(0, steps, one_step, 0)

    def faces_gone(up_rows):
        @pl.when(has_above)
        def _():
            for sim in range(2):
                for lo in pieces(up_rows):
                    up_copy(0, sim, lo, up_rows).wait_send()

    by_side(lambda: faces_gone(FAR_ROWS), lambda: faces_gone(width_y))
    lax.fori_loop(1, slabs, tiles_gone, 0)

    def add_shares(parts):
        for k in range(1, port_devices):
            for group, layers in enumerate(parts):
                share_copy(k, group, layers).wait_recv()
        total = summed[:, share_span(port)]
        for k in range(1, port_devices):
            total = total + shares[k]
        result[...] = total * (1.0 / math.sqrt(ports_ref.shape[1] * steps))
        for k in range(1, port_devices):
            for group, layers in enumerate(parts):
                share_copy(k, group, layers).wait_send()

    by_side(
        lambda: add_shares((pl.ds(0, last), pl.ds(last, 1))),
        lambda: add_shares((pl.ds(1, last), pl.ds(0, 1))))


def store_kernel(elec, magn, total, out_fields, out_sens, sem):
    rows = out_fields.shape[4]
    copies = [pltpu.make_async_copy(total, out_sens, sem.at[0])]
    for sim in range(2):
        for comp in range(3):
            copies.append(pltpu.make_async_copy(
                elec.at[sim, comp, :, pl.ds(0, rows)], out_fields.at[sim, 0, comp], sem.at[len(copies)]))
            copies.append(pltpu.make_async_copy(
                magn.at[sim, comp, :, pl.ds(PAD, rows)], out_fields.at[sim, 0, 3 + comp], sem.at[len(copies)]))
    for copy in copies:
        copy.start()
    for copy in copies:
        copy.wait()


def solution(mesh):
    slabs, port_devices = mesh.shape["space"], mesh.shape["port"]

    def local(fields, inv_eps, tensor_tiles, tile_index, ports, waves):
        assert fields.shape[1] == 1
        width_x, width_y, width_z = fields.shape[3:]
        steps = waves.shape[2]
        slots = tile_index.shape[2]
        owner_rows = tensor_tiles.shape[2]
        share_rows = width_y // port_devices
        far_pieces = width_y // FAR_ROWS
        f32 = jnp.float32
        dma = pltpu.SemaphoreType.DMA
        held = pl.BlockSpec(memory_space=pltpu.HBM)
        onchip = pl.BlockSpec(memory_space=pltpu.VMEM)
        anywhere = pl.BlockSpec(memory_space=pl.ANY)
        state = pl.pallas_call(
            functools.partial(kernel, slabs, port_devices),
            out_shape=(
                pltpu.VMEM((2, 3, width_x, width_y + PAD, width_z), f32),
                pltpu.VMEM((2, 3, width_x, width_y + PAD, width_z), f32),
                pltpu.VMEM((width_x, share_rows, width_z), f32),
            ),
            in_specs=[held] * 6,
            out_specs=(onchip, onchip, onchip),
            scratch_shapes=[
                pltpu.SMEM(ports.shape, jnp.int32),
                pltpu.SMEM(waves.shape, f32),
                pltpu.VMEM((steps, 2, 2, width_y, width_z), f32),
                pltpu.VMEM((steps, 2, 2, width_y, width_z), f32),
                pltpu.VMEM((2, 2, width_y, width_z), f32),
                pltpu.VMEM((6, 3 * slabs * slots, width_z), jnp.bfloat16),
                pltpu.VMEM((6, width_x, width_y, width_z), f32),
                pltpu.VMEM((3, width_x, width_y, width_z), f32),
                pltpu.VMEM((slabs * owner_rows, width_z), f32),
                pltpu.VMEM((slots, slabs), jnp.int32),
                pltpu.VMEM((width_x * width_y, 3 * slabs * slots), jnp.bfloat16),
                pltpu.VMEM((width_x * width_y, width_z), f32),
                pltpu.VMEM((width_x, width_y, width_z), f32),
                pltpu.VMEM((port_devices, width_x, share_rows, width_z), f32),
                dma((7,)),
                dma((slabs,)),
                dma((slabs,)),
                dma((2, far_pieces)),
                dma((steps, 2, far_pieces)),
                dma((2, far_pieces)),
                dma((steps, 2, far_pieces)),
                dma((port_devices, 2)),
                dma((port_devices, 2)),
                pltpu.SemaphoreType.REGULAR((GROUPS,)),
                pltpu.SemaphoreType.REGULAR,
            ],
            compiler_params=pltpu.CompilerParams(
                collective_id=0, has_side_effects=True, vmem_limit_bytes=40 * 1024 * 1024),
            name="window",
        )(*[pltpu.with_memory_space_constraint(x, pltpu.HBM) for x in (ports, waves, fields, inv_eps, tensor_tiles, tile_index.transpose(0, 2, 1))])
        return pl.pallas_call(
            store_kernel,
            out_shape=(
                jax.ShapeDtypeStruct(fields.shape, f32),
                jax.ShapeDtypeStruct((width_x, share_rows, width_z), f32),
            ),
            in_specs=[anywhere] * 3,
            out_specs=(anywhere, anywhere),
            scratch_shapes=[dma((13,))],
            compiler_params=pltpu.CompilerParams(vmem_limit_bytes=4 * 1024 * 1024),
            name="store",
        )(*[pltpu.with_memory_space_constraint(x, pltpu.VMEM) for x in state])

    in_specs = (
        P(None, "port", None, "space", None, None),
        P(None, "space", None, None),
        P("space", None, None, None),
        P("space", None, None),
        P(),
        P(None, "port", None),
    )
    out_specs = (P(None, "port", None, "space", None, None), P("space", "port", None))
    return jax.shard_map(local, mesh=mesh, in_specs=in_specs, out_specs=out_specs, check_vma=False)
```
